32 devices in a mesh: dp: 8 (over y, x, core), expert: 4 (over z).
Axes of the slice: x: 2, y: 2, z: 4, core: 2. Of those that a mesh axis runs over, the one named last changes fastest.
Arguments:
- tokens: bfloat16 [4096, 1280], P(('dp', 'expert')), may hold values from -6 to 6
- cotangent: bfloat16 [4096, 1280], P(('dp', 'expert')), may hold values from -4 to 4
- gate_weights: float32 [4096, 2], P(('dp', 'expert')), may hold values from 0.1 to 1
- expert_ids: int32 [4096, 2], P(('dp', 'expert')), may hold values from 0 to 7, as said below
- segments: int32 [32, 128], P(('dp', 'expert')), may hold values from 0 to 3, never falling along the last dimension, each value on 1 to 64 neighbouring positions
- keep_counts: int32 [32, 4], P(('dp', 'expert')), may hold values from 1 to 64
- expand_weight: bfloat16 [8, 2560, 1280], P('expert', 'dp'), may hold values from -0.15625 to 0.15625
- reduce_weight: bfloat16 [8, 2560, 1280], P('expert', 'dp'), may hold values from -0.125 to 0.125
Outputs:
- output: bfloat16 [4096, 1280], P(('dp', 'expert'))
- tokens_grad: bfloat16 [4096, 1280], P(('dp', 'expert'))
- gating_grad: float32 [4096, 2], P(('dp', 'expert'))
- expand_grad: bfloat16 [8, 2560, 1280], P('expert', 'dp')
- reduce_grad: bfloat16 [8, 2560, 1280], P('expert', 'dp')
The draws below stay inside these ranges and needn't reach their ends.
Inputs may be any that keep to these rules, and one draw needn't show every extreme that they name: `expert_ids`: the 128 tokens of one sequence name each expert exactly 32 times, and a token's 2 experts differ. `segments`: within a sequence the ids never fall, every image 0 to 3 appears, each holds 1 to 64 positions.
All inputs are finite; a program needn't handle non-finite values.
Results may differ from the reference program's by a relative error of at most 0.015.
Values may be sent and summed in bfloat16 or wider, within the bound.
No kernel may reach another device: no remote copies, remote signals or barrier semaphores. Data moves between devices by JAX's collectives and lax.ppermute only.
A program may use at most 128 MiB of HBM per device.

```python
import math
import jax
import jax.numpy as jnp
import numpy as np
from jax import lax

D = 1280
H = 2560
TOP = 2
IMGS = 4
TOK_DEV = 128
E = 8
SEG_MOST = 64
SEQS = 32
TOKENS = 4096
N_DP = 8
N_EXPERT = 4


def route_block(block_key):
    label_key, shift_key, flip_key, order_key = jax.random.split(block_key, 4)
    labels = jax.random.permutation(label_key, jnp.arange(E, dtype=jnp.int32))
    rounds = TOK_DEV // E
    shifts = jax.random.randint(shift_key, (rounds,), 1, E, dtype=jnp.int32)
    row_index = jnp.arange(TOK_DEV, dtype=jnp.int32)
    first_label = row_index % E
    second_label = (first_label + shifts[row_index // E]) % E
    first_ids = labels[first_label]
    second_ids = labels[second_label]
    flips = jax.random.randint(flip_key, (TOK_DEV,), 0, 2, dtype=jnp.int32)
    column_zero = jnp.where(flips == 1, second_ids, first_ids)
    column_one = jnp.where(flips == 1, first_ids, second_ids)
    paired = jnp.stack([column_zero, column_one], axis=1)
    order = jax.random.permutation(order_key, jnp.arange(TOK_DEV, dtype=jnp.int32))
    return paired[order]


def draw_expert_ids(key, part):
    block_keys = jax.random.split(jax.random.fold_in(key, 7), SEQS)
    blocks = jax.vmap(route_block)(block_keys)
    return blocks.reshape(TOKENS, TOP).astype(jnp.int32)


def touch_ends(values, stream_key, smallest, top_value):
    extent = values.shape
    spot = [jax.random.randint(jax.random.fold_in(stream_key, axis), (), 0, extent[axis]) for axis in range(len(extent))]
    values = values.at[tuple(spot)].set(smallest)
    longest = extent.index(max(extent))
    spot[longest] = (spot[longest] + 1) % extent[longest]
    return values.at[tuple(spot)].set(top_value)


def levels(key, shape, shards, smallest, largest):
    level = 1.0
    for dim, blocks in shards:
        steps = jax.random.uniform(jax.random.fold_in(jax.random.fold_in(key, 6), dim), (blocks,), jnp.float32, smallest / len(shards), largest / len(shards))
        level = level * jnp.repeat(jnp.exp(steps), shape[dim] // blocks).reshape((-1,) + (1,) * (len(shape) - 1 - dim))
    return level


def length_profile(count, total, most, lean):
    portions = [(1 << 20) // math.isqrt(rank ** lean) + 1 for rank in range(2, count + 1)]
    rest, holding = total - most - (count - 1), [1] * (count - 1)
    while rest > 0:
        movable = [i for i in range(count - 1) if holding[i] < most]
        whole, left = sum([portions[i] for i in movable]), rest
        for i in movable:
            more = min(most - holding[i], max(1, left * portions[i] // whole), rest)
            holding[i] = holding[i] + more
            rest = rest - more
    return np.array([most] + holding)


def ragged(own_key, number_of, total, most, slope):
    if number_of == 2:
        one = jax.random.randint(own_key, (), max(1, total - most), min(most, total - 1) + 1)
        return jnp.stack([one, total - one])
    tallies = jnp.asarray(length_profile(number_of, total, most, slope), jnp.int32)
    couples = (number_of - 1) // 2
    giver, receiver = tallies[1:1 + 2 * couples:2], tallies[2:2 + 2 * couples:2]
    margin = jnp.minimum(giver - 1, most - receiver)
    shifted = jax.random.randint(jax.random.fold_in(own_key, 1), (couples,), 0, 1 << 20) % (margin + 1)
    tallies = tallies.at[1:1 + 2 * couples:2].set(giver - shifted).at[2:2 + 2 * couples:2].set(receiver + shifted)
    return tallies[jax.random.permutation(jax.random.fold_in(own_key, 2), number_of)]


def noise(stream_key, extent, spread, reach, pieces=(), kind=jnp.bfloat16):
    loudness = levels(stream_key, extent, pieces, -0.22, 0.18) if pieces else 1.0
    drawn = jax.random.normal(stream_key, extent, jnp.float32) * spread * loudness
    return jnp.minimum(jnp.maximum(drawn, -reach), reach).astype(kind)


def setup_inputs(seed: int = 0) -> dict:
    streams_of = jax.random.split(jax.random.key(seed), 9)
    return {
        "tokens": noise(streams_of[0], (TOKENS, D), 1.0, 6.0, ((0, 32),)),
        "cotangent": noise(streams_of[1], (TOKENS, D), 0.3, 4.0, ((0, 32),)),
        "gate_weights": jnp.clip(0.1 + 0.9 * jax.random.uniform(streams_of[2], (TOKENS, TOP), jnp.float32) ** levels(streams_of[2], (TOKENS, TOP), ((0, 32),), -0.2, 0.2), 0.1, 1.0),
        "expert_ids": draw_expert_ids(jax.random.fold_in(streams_of[8], 71), 0),
        "segments": jax.vmap(lambda own: jnp.searchsorted(jnp.cumsum(ragged(own, IMGS, TOK_DEV, SEG_MOST, 1)), jnp.arange(TOK_DEV), side="right"))(jax.random.split(streams_of[4], SEQS)).reshape((SEQS, TOK_DEV)).astype(jnp.int32),
        "keep_counts": touch_ends(jax.random.randint(streams_of[5], (SEQS, IMGS), 1, SEG_MOST + 1), jax.random.fold_in(streams_of[5], 1), 1, SEG_MOST).astype(jnp.int32),
        "expand_weight": noise(streams_of[6], (E, H, D), D ** -0.5, 0.15625, ((0, 4), (1, 8))),
        "reduce_weight": noise(streams_of[7], (E, H, D), H ** -0.5, 0.125, ((0, 4), (1, 8))),
    }


epsilon = 1e-06
root_half = 0.7071067811865476
density_scale = 0.3989422804014327

def gelu_value(values):
    return 0.5 * values * (1.0 + jax.scipy.special.erf(values * root_half))

def gelu_slope(values):
    return 0.5 * (1.0 + jax.scipy.special.erf(values * root_half)) + values * jnp.exp(-0.5 * values * values) * density_scale

def round_partials(partials):
    return lax.optimization_barrier(partials.astype(jnp.bfloat16)).astype(jnp.float32)

def reference(tokens, cotangent, gate_weights, expert_ids, segments, keep_counts, expand_weight, reduce_weight):
    device_count = N_DP * N_EXPERT
    capacity = TOP * TOK_DEV // E
    position = jnp.arange(TOK_DEV, dtype=jnp.int32)
    earlier_img = lax.optimization_barrier(jnp.sum((segments[:, None, :] < segments[:, :, None]).astype(jnp.int32), axis=2))
    keep_token = jnp.take_along_axis(keep_counts, segments, axis=1)
    alive = (position[None, :] - earlier_img < keep_token).astype(jnp.float32).reshape(-1)
    tokens_wide = tokens.astype(jnp.float32)
    mean_rows = lax.optimization_barrier(jnp.mean(tokens_wide, axis=1, keepdims=True))
    centred = tokens_wide - mean_rows
    inv_scale = lax.rsqrt(lax.optimization_barrier(jnp.mean(centred * centred, axis=1, keepdims=True)) + epsilon)
    normed = centred * inv_scale
    normed_low = normed.astype(jnp.bfloat16)
    choice_list = expert_ids.reshape(device_count, TOP * TOK_DEV)
    matches = (choice_list[:, :, None] == jnp.arange(E, dtype=jnp.int32)[None, None, :]).astype(jnp.int32)
    before = jnp.cumsum(matches, axis=1) - matches
    slot_list = lax.optimization_barrier(jnp.sum(before * matches, axis=2)).reshape(-1).astype(jnp.int32)
    choice_flat = choice_list.reshape(-1).astype(jnp.int32)
    device_flat = jnp.repeat(jnp.arange(device_count, dtype=jnp.int32), TOP * TOK_DEV)
    alive_pick = jnp.repeat(alive, TOP)
    weight_pick = gate_weights.reshape(-1) * alive_pick
    feature_rows = jnp.where(alive_pick[:, None] > 0, jnp.repeat(normed_low, TOP, axis=0), jnp.zeros((), jnp.bfloat16))
    grad_rows = (jnp.repeat(cotangent.astype(jnp.float32), TOP, axis=0) * weight_pick[:, None]).astype(jnp.bfloat16)
    routed = jnp.zeros((device_count, E, capacity, D), jnp.bfloat16).at[device_flat, choice_flat, slot_list].set(feature_rows)
    routed_grad = jnp.zeros((device_count, E, capacity, D), jnp.bfloat16).at[device_flat, choice_flat, slot_list].set(grad_rows)

    def per_expert(inputs):
        features, grads, first, second = inputs
        features = features.reshape(-1, D)
        grads = grads.reshape(-1, D)
        pre = jnp.dot(features, first.T, preferred_element_type=jnp.float32)
        hidden = gelu_value(pre).astype(jnp.bfloat16)
        result = jnp.dot(hidden, second, preferred_element_type=jnp.float32).astype(jnp.bfloat16)
        back_hidden = jnp.dot(grads, second.T, preferred_element_type=jnp.float32)
        dpre = (back_hidden * gelu_slope(pre)).astype(jnp.bfloat16)
        input_rows = jnp.dot(dpre, first, preferred_element_type=jnp.float32).astype(jnp.bfloat16)
        hidden_blocks = hidden.reshape(N_DP, -1, H).astype(jnp.float32)
        dpre_blocks = dpre.reshape(N_DP, -1, H).astype(jnp.float32)
        grad_blocks = grads.reshape(N_DP, -1, D).astype(jnp.float32)
        feature_blocks = features.reshape(N_DP, -1, D).astype(jnp.float32)
        second_parts = jnp.einsum('bsh,bsd->bhd', hidden_blocks, grad_blocks)
        first_parts = jnp.einsum('bsh,bsd->bhd', dpre_blocks, feature_blocks)
        second_grad = lax.optimization_barrier(jnp.sum(round_partials(second_parts), axis=0)).astype(jnp.bfloat16)
        first_grad = lax.optimization_barrier(jnp.sum(round_partials(first_parts), axis=0)).astype(jnp.bfloat16)
        return (result, input_rows, first_grad, second_grad)
    results, input_grads, expand_grad, reduce_grad = lax.map(per_expert, (routed.transpose(1, 0, 2, 3), routed_grad.transpose(1, 0, 2, 3), expand_weight, reduce_weight))
    results = results.reshape(E, device_count, capacity, D)
    input_grads = input_grads.reshape(E, device_count, capacity, D)
    result_pick = results[choice_flat, device_flat, slot_list].astype(jnp.float32).reshape(-1, TOP, D)
    input_pick = input_grads[choice_flat, device_flat, slot_list].astype(jnp.float32).reshape(-1, TOP, D)
    output = (tokens_wide + lax.optimization_barrier(jnp.sum(result_pick * weight_pick.reshape(-1, TOP, 1), axis=1))).astype(jnp.bfloat16)
    cot_wide = cotangent.astype(jnp.float32)
    gating_grad = alive_pick.reshape(-1, TOP) * lax.optimization_barrier(jnp.sum(cot_wide[:, None, :] * result_pick, axis=2))
    grad_norm = lax.optimization_barrier(jnp.sum(input_pick * alive_pick.reshape(-1, TOP, 1), axis=1))
    tokens_grad = cot_wide + inv_scale * (grad_norm - lax.optimization_barrier(jnp.mean(grad_norm, axis=1, keepdims=True)) - normed * lax.optimization_barrier(jnp.mean(grad_norm * normed, axis=1, keepdims=True)))
    return (output, tokens_grad.astype(jnp.bfloat16), gating_grad, expand_grad, reduce_grad)
```

```python
import functools

import jax
import jax.numpy as jnp
from jax import lax
from jax.experimental import pallas as pl
from jax.experimental.pallas import tpu as pltpu
from jax.sharding import PartitionSpec as P

epsilon = 1e-06
root_half = 0.7071067811865476
density_scale = 0.3989422804014327


def dot(left, right, left_dim, right_dim):
    return lax.dot_general(
        left, right, (((left_dim,), (right_dim,)), ((), ())), preferred_element_type=jnp.float32
    )


def normalize(tokens):
    wide = tokens.astype(jnp.float32)
    centred = wide - jnp.mean(wide, axis=1, keepdims=True)
    inv_scale = lax.rsqrt(jnp.mean(centred * centred, axis=1, keepdims=True) + epsilon)
    return centred * inv_scale, inv_scale


def one_hot(target, rows):
    lanes = lax.broadcasted_iota(jnp.int32, (target.shape[0], rows), 1)
    return (target == lanes).astype(jnp.bfloat16)


def route_kernel(
    planes, local, me_ref, tok_ref, cot_ref, gate_ref, ids_ref, seg_ref, keep_ref, *outs
):
    toks, top = ids_ref.shape
    experts = planes * local
    cap = top * toks // experts
    feature_refs = [outs[l * planes : (l + 1) * planes] for l in range(local)]
    grad_refs = outs[local * planes : (local + 1) * planes]
    target_ref, weight_ref, alive_ref = outs[(local + 1) * planes :]
    seg = seg_ref[...]
    spot = lax.broadcasted_iota(jnp.int32, seg.shape, 1).astype(jnp.float32)
    alive_row = jnp.zeros(seg.shape, jnp.float32)
    for image in range(keep_ref.shape[1]):
        start = jnp.sum((seg < image).astype(jnp.float32), axis=1, keepdims=True)
        limit = keep_ref[0:1, image : image + 1].astype(jnp.float32)
        alive_row = jnp.where((seg == image) & (spot - start < limit), 1.0, alive_row)
    row = lax.broadcasted_iota(jnp.int32, (toks, toks), 0)
    col = lax.broadcasted_iota(jnp.int32, (toks, toks), 1)
    alive = jnp.sum(jnp.where(row == col, alive_row, 0.0), axis=1, keepdims=True)
    ids = ids_ref[...]
    width = -(-experts // 128) * 128
    lanes = lax.broadcasted_iota(jnp.int32, (toks, width), 1)
    chosen = [(ids[:, k : k + 1] == lanes).astype(jnp.float32) for k in range(top)]
    every = chosen[0]
    for k in range(1, top):
        every = every + chosen[k]
    before = dot((col < row).astype(jnp.bfloat16), every.astype(jnp.bfloat16), 1, 0)
    me = me_ref[0]
    hots = []
    scaled = []
    cot = cot_ref[...].astype(jnp.float32)
    for k in range(top):
        expert = ids[:, k : k + 1]
        slot = jnp.sum(before * chosen[k], axis=1, keepdims=True).astype(jnp.int32)
        away = jnp.bitwise_xor(lax.div(expert, local), me)
        target = (away * local + lax.rem(expert, local)) * cap + slot
        weight = gate_ref[:, k : k + 1] * alive
        target_ref[:, k : k + 1] = target
        weight_ref[:, k : k + 1] = weight
        hots.append(one_hot(target, experts * cap))
        scaled.append((cot * weight).astype(jnp.bfloat16))
    alive_ref[...] = alive
    normed, _ = normalize(tok_ref[...])
    low = jnp.where(alive > 0, normed, 0.0).astype(jnp.bfloat16)
    every_hot = hots[0]
    for k in range(1, top):
        every_hot = every_hot + hots[k]
    features = dot(every_hot, low, 0, 0).astype(jnp.bfloat16)
    grads = dot(jnp.concatenate(hots, 0), jnp.concatenate(scaled, 0), 0, 0).astype(jnp.bfloat16)
    for away in range(planes):
        base = away * local * cap
        grad_refs[away][...] = grads[base : base + local * cap]
        for l in range(local):
            feature_refs[l][away][...] = features[base + l * cap : base + (l + 1) * cap]


def forward_kernel(blocks, send_slots, *refs):
    rows_refs = refs[:blocks]
    up_own, up_pair, down_own, down_pair, send_ref, keep_ref, hidden_ref, slope_ref = refs[blocks:]
    rows = jnp.concatenate([ref[...] for ref in rows_refs], 0)
    up = jnp.concatenate([up_own[0], up_pair[0]], 0)
    pre = dot(rows, up, 1, 1)
    half = 0.5 * (1.0 + lax.erf(pre * root_half))
    hidden = (pre * half).astype(jnp.bfloat16)
    hidden_ref[...] = hidden
    slope_ref[...] = half + pre * jnp.exp(-0.5 * pre * pre) * density_scale
    down = jnp.concatenate([down_own[0], down_pair[0]], 0)
    spread(dot(hidden, down, 1, 0), send_slots, send_ref, keep_ref)


def spread(result, send_slots, send_ref, keep_ref):
    block_rows = keep_ref.shape[1]
    for index, slots in enumerate(send_slots):
        for ref, block in zip((send_ref, keep_ref), slots):
            ref[index] = result[block * block_rows : (block + 1) * block_rows].astype(jnp.bfloat16)


def backward_kernel(blocks, send_slots, *refs):
    grad_refs = refs[:blocks]
    up_own, up_pair, down_own, down_pair, slope_ref, send_ref, keep_ref, dpre_ref = refs[blocks:]
    grads = jnp.concatenate([ref[...] for ref in grad_refs], 0)
    down = jnp.concatenate([down_own[0], down_pair[0]], 0)
    dpre = (dot(grads, down, 1, 1) * slope_ref[...]).astype(jnp.bfloat16)
    dpre_ref[...] = dpre
    up = jnp.concatenate([up_own[0], up_pair[0]], 0)
    spread(dot(dpre, up, 1, 0), send_slots, send_ref, keep_ref)


def weight_kernel(blocks, *refs):
    rows_refs = refs[:blocks]
    grad_refs = refs[blocks : 2 * blocks]
    hidden_ref, dpre_ref, own_ref, pair_ref = refs[2 * blocks :]
    units = own_ref.shape[1]
    for index, (left_ref, right_refs) in enumerate(
        ((dpre_ref, rows_refs), (hidden_ref, grad_refs))
    ):
        right = jnp.concatenate([ref[...] for ref in right_refs], 0)
        product = dot(left_ref[...], right, 0, 0)
        own_ref[index] = product[:units].astype(jnp.bfloat16)
        pair_ref[index] = product[units:].astype(jnp.bfloat16)


def total_kernel(local, *refs):
    own_refs = refs[:local]
    pair_refs = refs[local : 2 * local]
    out_refs = refs[2 * local :]
    for l in range(local):
        for index, ref in enumerate(out_refs):
            ref[l] = (
                own_refs[l][index].astype(jnp.float32) + pair_refs[l][index].astype(jnp.float32)
            ).astype(jnp.bfloat16)


def finish_kernel(counts, planes, *refs):
    used = sum(counts)
    outs = refs[used:]
    cap = outs[0].shape[0] // len(counts)
    start = 0
    for l, count in enumerate(counts):
        total = refs[start][0].astype(jnp.float32)
        for ref in refs[start + 1 : start + count]:
            total = total + ref[0].astype(jnp.float32)
        start += count
        low = total.astype(jnp.bfloat16)
        for away in range(planes):
            outs[away][l * cap : (l + 1) * cap] = low[away * cap : (away + 1) * cap]


def output_kernel(planes, *refs):
    result_refs = refs[:planes]
    tok_ref, cot_ref, target_ref, weight_ref, alive_ref, out_ref, gating_ref = refs[planes:]
    results = jnp.concatenate([ref[...] for ref in result_refs], 0)
    total = tok_ref[...].astype(jnp.float32)
    cot = cot_ref[...].astype(jnp.float32)
    for k in range(target_ref.shape[1]):
        picked = dot(one_hot(target_ref[:, k : k + 1], results.shape[0]), results, 1, 0)
        total = total + weight_ref[:, k : k + 1] * picked
        gating_ref[:, k : k + 1] = alive_ref[...] * jnp.sum(cot * picked, axis=1, keepdims=True)
    out_ref[...] = total.astype(jnp.bfloat16)


def input_kernel(planes, local, *refs):
    grad_refs = refs[: planes * local]
    tok_ref, cot_ref, target_ref, alive_ref, out_ref = refs[planes * local :]
    grads = jnp.concatenate([ref[...] for ref in grad_refs], 0)
    hot = one_hot(target_ref[:, 0:1], grads.shape[0])
    for k in range(1, target_ref.shape[1]):
        hot = hot + one_hot(target_ref[:, k : k + 1], grads.shape[0])
    dnorm = alive_ref[...] * dot(hot, grads, 1, 0)
    normed, inv_scale = normalize(tok_ref[...])
    inner = jnp.mean(dnorm * normed, axis=1, keepdims=True)
    change = dnorm - jnp.mean(dnorm, axis=1, keepdims=True) - normed * inner
    out_ref[...] = (cot_ref[...].astype(jnp.float32) + inv_scale * change).astype(jnp.bfloat16)


def whole(array):
    rank = len(array.shape)
    return pl.BlockSpec(array.shape, lambda *_: (0,) * rank)


def part(array, index):
    rank = len(array.shape)
    return pl.BlockSpec((1,) + array.shape[1:], lambda *_: (index,) + (0,) * (rank - 1))


def run(kernel, inputs, outs, name):
    arrays = [item[0] if isinstance(item, tuple) else item for item in inputs]
    specs = [part(*item) if isinstance(item, tuple) else whole(item) for item in inputs]
    outs = [jax.ShapeDtypeStruct(shape, dtype) for shape, dtype in outs]
    return pl.pallas_call(
        kernel,
        out_shape=outs,
        grid=(1,),
        in_specs=specs,
        out_specs=[whole(out) for out in outs],
        compiler_params=pltpu.CompilerParams(vmem_limit_bytes=40 << 20),
        name=name,
    )(*arrays)


def body(
    tokens, cotangent, gate_weights, expert_ids, segments, keep_counts, expand_weight, reduce_weight
):
    toks, width = tokens.shape
    top = expert_ids.shape[1]
    groups = lax.axis_size("dp")
    planes = lax.axis_size("expert")
    local, units, _ = expand_weight.shape
    cap = top * toks // (planes * local)
    blocks = groups // 2
    bits = [1 << bit for bit in range(1, groups.bit_length() - 1)]
    low = jnp.bfloat16

    def swap(values, mask):
        return lax.ppermute(values, "dp", [(i, i ^ mask) for i in range(groups)])

    def cross(values, mask):
        return lax.ppermute(values, "expert", [(i, i ^ mask) for i in range(planes)])

    def order_of(index):
        shift = index % len(bits)
        return bits[shift:] + bits[:shift]

    def gather(own, order):
        held = {0: own}
        for bit in order:
            for block in sorted(held):
                held[block | bit] = swap(held[block], bit)
        return [held[2 * index] for index in range(blocks)]

    def slots_of(order):
        bit = order[0] // 2
        return tuple((block | bit, block) for block in range(blocks) if not block & bit)

    def scatter(send, keep, order):
        bit = order[0]
        arrived = swap(send, bit)
        terms = {
            2 * slots[1]: [(keep, index), (arrived, index)]
            for index, slots in enumerate(slots_of(order))
        }
        for bit in order[1:]:
            leaving = [block for block in sorted(terms) if block & bit]
            sums = [
                sum(array[index].astype(jnp.float32) for array, index in terms[block]).astype(low)
                for block in leaving
            ]
            arrived = swap(jnp.stack(sums), bit)
            for index, block in enumerate(leaving):
                terms[block ^ bit].append((arrived, index))
            for block in leaving:
                del terms[block]
        return terms[0]

    up_pair = swap(expand_weight, 1)
    down_pair = swap(reduce_weight, 1)
    me = lax.axis_index("expert").astype(jnp.int32).reshape(1)
    narrow = (cap, width)
    routed = pl.pallas_call(
        functools.partial(route_kernel, planes, local),
        out_shape=[jax.ShapeDtypeStruct(narrow, low)] * (local * planes)
        + [jax.ShapeDtypeStruct((local * cap, width), low)] * planes
        + [
            jax.ShapeDtypeStruct((toks, top), jnp.int32),
            jax.ShapeDtypeStruct((toks, top), jnp.float32),
            jax.ShapeDtypeStruct((toks, 1), jnp.float32),
        ],
        in_specs=[pl.BlockSpec(memory_space=pltpu.SMEM)]
        + [pl.BlockSpec(memory_space=pltpu.VMEM)] * 6,
        compiler_params=pltpu.CompilerParams(vmem_limit_bytes=40 << 20),
        name="route",
    )(me, tokens, cotangent, gate_weights, expert_ids, segments, keep_counts)
    target, weight, alive = routed[-3:]

    features = []
    for l in range(local):
        pieces = routed[l * planes : (l + 1) * planes]
        own = jnp.concatenate([pieces[0]] + [cross(pieces[s], s) for s in range(1, planes)], 0)
        features.append(gather(own, order_of(l)))
    pieces = routed[local * planes : (local + 1) * planes]
    pieces = [pieces[0]] + [cross(pieces[s], s) for s in range(1, planes)]
    grads = [
        gather(
            jnp.concatenate([piece[l * cap : (l + 1) * cap] for piece in pieces], 0), order_of(l)
        )
        for l in range(local)
    ]

    rows = blocks * planes * cap
    halves = ((blocks // 2, planes * cap, width), low)
    hiddens, slopes, result_terms = [], [], []
    for l in range(local):
        send, keep, hidden, slope = run(
            functools.partial(forward_kernel, blocks, slots_of(order_of(l))),
            features[l]
            + [(expand_weight, l), (up_pair, l), (reduce_weight, l), (down_pair, l)],
            [halves, halves, ((rows, 2 * units), low), ((rows, 2 * units), jnp.float32)],
            "forward",
        )
        hiddens.append(hidden)
        slopes.append(slope)
        result_terms.append(scatter(send, keep, order_of(l)))
    dpres, input_terms = [], []
    for l in range(local):
        send, keep, dpre = run(
            functools.partial(backward_kernel, blocks, slots_of(order_of(l))),
            grads[l]
            + [(expand_weight, l), (up_pair, l), (reduce_weight, l), (down_pair, l), slopes[l]],
            [halves, halves, ((rows, 2 * units), low)],
            "backward",
        )
        dpres.append(dpre)
        input_terms.append(scatter(send, keep, order_of(l)))
    owns, pairs = [], []
    for l in range(local):
        own, pair = run(
            functools.partial(weight_kernel, blocks),
            features[l] + grads[l] + [hiddens[l], dpres[l]],
            [((2, units, width), low)] * 2,
            "weights",
        )
        owns.append(own)
        pairs.append(swap(pair, 1))
    expand_grad, reduce_grad = run(
        functools.partial(total_kernel, local),
        owns + pairs,
        [(expand_weight.shape, low)] * 2,
        "total",
    )

    def finish(terms_list, name):
        counts = [len(terms) for terms in terms_list]
        outs = run(
            functools.partial(finish_kernel, counts, planes),
            [item for terms in terms_list for item in terms],
            [((len(terms_list) * cap, width), low)] * planes,
            name,
        )
        return [outs[0]] + [cross(outs[s], s) for s in range(1, planes)]

    returned = finish(result_terms, "finish_results")
    output, gating_grad = run(
        functools.partial(output_kernel, planes),
        returned + [tokens, cotangent, target, weight, alive],
        [(tokens.shape, low), ((toks, top), jnp.float32)],
        "output",
    )
    back = [finish([terms], "finish_inputs") for terms in input_terms]
    (tokens_grad,) = run(
        functools.partial(input_kernel, planes, local),
        [back[l][s] for s in range(planes) for l in range(local)]
        + [tokens, cotangent, target, alive],
        [(tokens.shape, low)],
        "inputs",
    )
    return (output, tokens_grad, gating_grad, expand_grad, reduce_grad)


def solution(mesh):
    rows = P(("dp", "expert"), None)
    weights = P("expert", "dp", None)
    return jax.shard_map(
        body,
        mesh=mesh,
        in_specs=(rows,) * 6 + (weights,) * 2,
        out_specs=(rows,) * 3 + (weights,) * 2,
        check_vma=False,
    )
```

```python
import functools

import jax
import jax.numpy as jnp
from jax import lax
from jax.experimental import pallas as pl
from jax.experimental.pallas import tpu as pltpu
from jax.sharding import PartitionSpec as P

epsilon = 1e-06
root_half = 0.7071067811865476
density_scale = 0.3989422804014327


def dot(left, right, left_dim, right_dim):
    return lax.dot_general(
        left, right, (((left_dim,), (right_dim,)), ((), ())), preferred_element_type=jnp.float32
    )


def normalize(tokens):
    wide = tokens.astype(jnp.float32)
    centred = wide - jnp.mean(wide, axis=1, keepdims=True)
    inv_scale = lax.rsqrt(jnp.mean(centred * centred, axis=1, keepdims=True) + epsilon)
    return centred * inv_scale, inv_scale


def one_hot(target, rows):
    lanes = lax.broadcasted_iota(jnp.int32, (target.shape[0], rows), 1)
    return (target == lanes).astype(jnp.bfloat16)


def to_column(row, same):
    return jnp.sum(jnp.where(same, row, 0.0), axis=1, keepdims=True)


def route_kernel(
    planes, local, me_ref, tok_hbm, cot_hbm, gate_ref, ids_ref, seg_ref, keep_ref, *refs
):
    outs, (tok_ref, cot_ref, sems) = refs[:-3], refs[-3:]
    tok_copy = pltpu.make_async_copy(tok_hbm, tok_ref, sems.at[0])
    cot_copy = pltpu.make_async_copy(cot_hbm, cot_ref, sems.at[1])
    tok_copy.start()
    cot_copy.start()
    top, toks = ids_ref.shape
    experts = planes * local
    cap = top * toks // experts
    feature_refs = [outs[l * planes : (l + 1) * planes] for l in range(local)]
    grad_refs = outs[local * planes : (local + 1) * planes]
    target_ref, weight_ref, alive_ref = outs[(local + 1) * planes :]
    seg = seg_ref[...]
    spot = lax.broadcasted_iota(jnp.int32, seg.shape, 1).astype(jnp.float32)
    alive_row = jnp.zeros(seg.shape, jnp.float32)
    for image in range(keep_ref.shape[1]):
        start = jnp.sum((seg < image).astype(jnp.float32), axis=1, keepdims=True)
        limit = keep_ref[0:1, image : image + 1].astype(jnp.float32)
        alive_row = jnp.where((seg == image) & (spot - start < limit), 1.0, alive_row)
    row = lax.broadcasted_iota(jnp.int32, (toks, toks), 0)
    col = lax.broadcasted_iota(jnp.int32, (toks, toks), 1)
    same = row == col
    alive = to_column(alive_row, same)
    width = -(-experts // 128) * 128
    lanes = lax.broadcasted_iota(jnp.int32, (toks, width), 1)
    picks = [
        to_column(ids_ref[k : k + 1, :].astype(jnp.float32), same).astype(jnp.int32)
        for k in range(top)
    ]
    chosen = [(pick == lanes).astype(jnp.float32) for pick in picks]
    every = chosen[0]
    for k in range(1, top):
        every = every + chosen[k]
    before = dot((col < row).astype(jnp.bfloat16), every.astype(jnp.bfloat16), 1, 0)
    me = me_ref[0]
    hots = []
    weights = []
    for k in range(top):
        slot = jnp.sum(before * chosen[k], axis=1, keepdims=True).astype(jnp.int32)
        away = jnp.bitwise_xor(lax.div(picks[k], local), me)
        target = (away * local + lax.rem(picks[k], local)) * cap + slot
        weight = to_column(gate_ref[k : k + 1, :] * alive_row, same)
        target_ref[:, k : k + 1] = target
        weight_ref[:, k : k + 1] = weight
        hots.append(one_hot(target, experts * cap))
        weights.append(weight)
    alive_ref[...] = alive
    tok_copy.wait()
    normed, _ = normalize(tok_ref[...])
    low = jnp.where(alive > 0, normed, 0.0).astype(jnp.bfloat16)
    every_hot = hots[0]
    for k in range(1, top):
        every_hot = every_hot + hots[k]
    features = dot(every_hot, low, 0, 0).astype(jnp.bfloat16)
    for away in range(planes):
        base = away * local * cap
        for l in range(local):
            feature_refs[l][away][...] = features[base + l * cap : base + (l + 1) * cap]
    cot_copy.wait()
    cot = cot_ref[...].astype(jnp.float32)
    scaled = [(cot * weight).astype(jnp.bfloat16) for weight in weights]
    grads = dot(jnp.concatenate(hots, 0), jnp.concatenate(scaled, 0), 0, 0).astype(jnp.bfloat16)
    for away in range(planes):
        base = away * local * cap
        grad_refs[away][...] = grads[base : base + local * cap]


def join_kernel(planes, cap, *refs):
    piece_refs, outs = refs[:planes], refs[planes:]
    for l, out in enumerate(outs):
        for away, ref in enumerate(piece_refs):
            out[away * cap : (away + 1) * cap] = ref[l * cap : (l + 1) * cap]


def add_kernel(*refs):
    total = refs[0][0].astype(jnp.float32)
    for ref in refs[1:-1]:
        total = total + ref[0].astype(jnp.float32)
    refs[-1][0] = total.astype(jnp.bfloat16)


def forward_kernel(blocks, parts, *refs):
    rows_refs = refs[:blocks]
    up_own, up_pair, down_own, down_pair, hidden_ref, slope_ref = refs[blocks : blocks + 6]
    rows = jnp.concatenate([ref[...] for ref in rows_refs], 0)
    up = jnp.concatenate([up_own[0], up_pair[0]], 0)
    pre = dot(rows, up, 1, 1)
    half = 0.5 * (1.0 + lax.erf(pre * root_half))
    hidden = (pre * half).astype(jnp.bfloat16)
    hidden_ref[...] = hidden
    slope_ref[...] = half + pre * jnp.exp(-0.5 * pre * pre) * density_scale
    down = jnp.concatenate([down_own[0], down_pair[0]], 0)
    spread(dot(hidden, down, 1, 0), blocks, parts, refs[blocks + 6 :])


def spread(result, blocks, parts, refs):
    block_rows = result.shape[0] // blocks
    for number, (start, stop, slots) in enumerate(parts):
        for index, pair in enumerate(slots):
            for ref, block in zip(refs[2 * number : 2 * number + 2], pair):
                base = block * block_rows
                ref[index] = result[base + start : base + stop].astype(jnp.bfloat16)


def backward_kernel(blocks, parts, *refs):
    grad_refs = refs[:blocks]
    up_own, up_pair, down_own, down_pair, slope_ref, dpre_ref = refs[blocks : blocks + 6]
    grads = jnp.concatenate([ref[...] for ref in grad_refs], 0)
    down = jnp.concatenate([down_own[0], down_pair[0]], 0)
    dpre = (dot(grads, down, 1, 1) * slope_ref[...]).astype(jnp.bfloat16)
    dpre_ref[...] = dpre
    up = jnp.concatenate([up_own[0], up_pair[0]], 0)
    spread(dot(dpre, up, 1, 0), blocks, parts, refs[blocks + 6 :])


def weight_kernel(blocks, *refs):
    rows_refs = refs[:blocks]
    grad_refs = refs[blocks : 2 * blocks]
    hidden_ref, dpre_ref, own_ref, pair_ref = refs[2 * blocks :]
    units = own_ref.shape[1]
    for index, (left_ref, right_refs) in enumerate(
        ((dpre_ref, rows_refs), (hidden_ref, grad_refs))
    ):
        right = jnp.concatenate([ref[...] for ref in right_refs], 0)
        product = dot(left_ref[...], right, 0, 0)
        own_ref[index] = product[:units].astype(jnp.bfloat16)
        pair_ref[index] = product[units:].astype(jnp.bfloat16)


def total_kernel(local, *refs):
    own_refs = refs[:local]
    pair_refs = refs[local : 2 * local]
    out_refs = refs[2 * local :]
    for l in range(local):
        for index, ref in enumerate(out_refs):
            ref[l] = (
                own_refs[l][index].astype(jnp.float32) + pair_refs[l][index].astype(jnp.float32)
            ).astype(jnp.bfloat16)


def finish_kernel(groups, *refs):
    outs = refs[sum(count for counts in groups for count in counts) :]
    cap = outs[0].shape[0] // len(groups)
    used = 0
    for l, counts in enumerate(groups):
        away = 0
        for count in counts:
            total = refs[used][0].astype(jnp.float32)
            for ref in refs[used + 1 : used + count]:
                total = total + ref[0].astype(jnp.float32)
            used += count
            low = total.astype(jnp.bfloat16)
            for index in range(low.shape[0] // cap):
                outs[away][l * cap : (l + 1) * cap] = low[index * cap : (index + 1) * cap]
                away += 1


def output_kernel(planes, *refs):
    result_refs = refs[:planes]
    tok_ref, cot_ref, target_ref, weight_ref, alive_ref, out_ref, gating_ref = refs[planes:]
    results = jnp.concatenate([ref[...] for ref in result_refs], 0)
    toks = tok_ref.shape[0]
    row = lax.broadcasted_iota(jnp.int32, (toks, toks), 0)
    same = row == lax.broadcasted_iota(jnp.int32, (toks, toks), 1)
    total = tok_ref[...].astype(jnp.float32)
    cot = cot_ref[...].astype(jnp.float32)
    for k in range(target_ref.shape[1]):
        picked = dot(one_hot(target_ref[:, k : k + 1], results.shape[0]), results, 1, 0)
        total = total + weight_ref[:, k : k + 1] * picked
        column = alive_ref[...] * jnp.sum(cot * picked, axis=1, keepdims=True)
        gating_ref[k : k + 1, :] = jnp.sum(jnp.where(same, column, 0.0), axis=0, keepdims=True)
    out_ref[...] = total.astype(jnp.bfloat16)


def input_kernel(planes, local, *refs):
    grad_refs = refs[: planes * local]
    tok_ref, cot_ref, target_ref, alive_ref, out_ref = refs[planes * local :]
    grads = jnp.concatenate([ref[...] for ref in grad_refs], 0)
    hot = one_hot(target_ref[:, 0:1], grads.shape[0])
    for k in range(1, target_ref.shape[1]):
        hot = hot + one_hot(target_ref[:, k : k + 1], grads.shape[0])
    dnorm = alive_ref[...] * dot(hot, grads, 1, 0)
    normed, inv_scale = normalize(tok_ref[...])
    inner = jnp.mean(dnorm * normed, axis=1, keepdims=True)
    change = dnorm - jnp.mean(dnorm, axis=1, keepdims=True) - normed * inner
    out_ref[...] = (cot_ref[...].astype(jnp.float32) + inv_scale * change).astype(jnp.bfloat16)


def whole(array):
    rank = len(array.shape)
    return pl.BlockSpec(array.shape, lambda *_: (0,) * rank)


def part(array, index):
    rank = len(array.shape)
    return pl.BlockSpec((1,) + array.shape[1:], lambda *_: (index,) + (0,) * (rank - 1))


def run(kernel, inputs, outs):
    arrays = [item[0] if isinstance(item, tuple) else item for item in inputs]
    specs = [part(*item) if isinstance(item, tuple) else whole(item) for item in inputs]
    outs = [jax.ShapeDtypeStruct(shape, dtype) for shape, dtype in outs]
    return pl.pallas_call(
        kernel,
        out_shape=outs,
        grid=(1,),
        in_specs=specs,
        out_specs=[whole(out) for out in outs],
        compiler_params=pltpu.CompilerParams(vmem_limit_bytes=40 << 20),
    )(*arrays)


def body(
    tokens, cotangent, gate_weights, expert_ids, segments, keep_counts, expand_weight, reduce_weight
):
    toks, width = tokens.shape
    top = expert_ids.shape[1]
    groups = lax.axis_size("dp")
    planes = lax.axis_size("expert")
    local, units, _ = expand_weight.shape
    cap = top * toks // (planes * local)
    blocks = groups // 2
    bits = [1 << bit for bit in range(1, groups.bit_length() - 1)]
    block_rows = planes * cap
    low = jnp.bfloat16

    def swap(values, mask):
        return lax.ppermute(values, "dp", [(i, i ^ mask) for i in range(groups)])

    def cross(pieces):
        away = []
        for s in range(1, planes):
            away.append(
                lax.ppermute(pieces[s], "expert", [(i, i ^ s) for i in range(planes)])
            )
        return [pieces[0]] + away

    def order_of(index):
        shift = index % len(bits)
        return bits[shift:] + bits[:shift]

    def gather(own, order):
        held = {0: own}
        for bit in order:
            for block in sorted(held):
                held[block | bit] = swap(held[block], bit)
        return [held[2 * index] for index in range(blocks)]

    def part_of(start, stop, order):
        bit = order[0] // 2
        slots = tuple((block | bit, block) for block in range(blocks) if not block & bit)
        return start, stop, slots

    def scatter(send, keep, order):
        bit = order[0]
        arrived = swap(send, bit)
        terms = {
            2 * slots[1]: [(keep, index), (arrived, index)]
            for index, slots in enumerate(part_of(0, 0, order)[2])
        }
        for bit in order[1:]:
            leaving = [block for block in sorted(terms) if block & bit]
            sums = [
                run(add_kernel, terms[block], [((1,) + send.shape[1:], low)])[0]
                for block in leaving
            ]
            sums = sums[0] if len(sums) == 1 else jnp.concatenate(sums, 0)
            arrived = swap(sums, bit)
            for index, block in enumerate(leaving):
                terms[block ^ bit].append((arrived, index))
                del terms[block]
        return terms[0]

    me = lax.axis_index("expert").astype(jnp.int32).reshape(1)
    routed = pl.pallas_call(
        functools.partial(route_kernel, planes, local),
        out_shape=[jax.ShapeDtypeStruct((cap, width), low)] * (local * planes)
        + [jax.ShapeDtypeStruct((local * cap, width), low)] * planes
        + [
            jax.ShapeDtypeStruct((toks, top), jnp.int32),
            jax.ShapeDtypeStruct((toks, top), jnp.float32),
            jax.ShapeDtypeStruct((toks, 1), jnp.float32),
        ],
        in_specs=[pl.BlockSpec(memory_space=pltpu.SMEM)]
        + [pl.BlockSpec(memory_space=pltpu.HBM)] * 2
        + [pl.BlockSpec(memory_space=pltpu.VMEM)] * 4,
        scratch_shapes=[
            pltpu.VMEM(tokens.shape, tokens.dtype),
            pltpu.VMEM(tokens.shape, tokens.dtype),
            pltpu.SemaphoreType.DMA((2,)),
        ],
        compiler_params=pltpu.CompilerParams(vmem_limit_bytes=40 << 20),
        name="route",
    )(me, tokens, cotangent, gate_weights.T, expert_ids.T, segments, keep_counts)
    target, weight, alive = routed[-3:]
    up_pair = swap(expand_weight, 1)
    down_pair = swap(reduce_weight, 1)

    features = []
    for l in range(local):
        pieces = cross(routed[l * planes : (l + 1) * planes])
        (own,) = run(
            functools.partial(join_kernel, planes, cap), pieces, [((block_rows, width), low)]
        )
        features.append(gather(own, order_of(l)))
    pieces = cross(routed[local * planes : (local + 1) * planes])
    owns = run(
        functools.partial(join_kernel, planes, cap), pieces, [((block_rows, width), low)] * local
    )
    grads = [gather(owns[l], order_of(l)) for l in range(local)]

    rows = blocks * block_rows

    def outs_of(parts):
        return [
            ((blocks // 2, stop - start, width), low) for start, stop, _ in parts for _ in range(2)
        ]

    hiddens, slopes, result_terms = [], [], []
    for l in range(local):
        parts = [part_of(0, block_rows, order_of(l))]
        hidden, slope, send, keep = run(
            functools.partial(forward_kernel, blocks, parts),
            features[l]
            + [(expand_weight, l), (up_pair, l), (reduce_weight, l), (down_pair, l)],
            [((rows, 2 * units), low), ((rows, 2 * units), jnp.float32)] + outs_of(parts),
        )
        hiddens.append(hidden)
        slopes.append(slope)
        result_terms.append([scatter(send, keep, order_of(l))])
    half = block_rows // 2
    dpres, input_terms = [], []
    for l in range(local):
        parts = [part_of(0, half, order_of(0)), part_of(half, block_rows, order_of(1))]
        dpre, *sends = run(
            functools.partial(backward_kernel, blocks, parts),
            grads[l]
            + [(expand_weight, l), (up_pair, l), (reduce_weight, l), (down_pair, l), slopes[l]],
            [((rows, 2 * units), low)] + outs_of(parts),
        )
        dpres.append(dpre)
        input_terms.append(
            [scatter(sends[2 * index], sends[2 * index + 1], order_of(index)) for index in range(2)]
        )
    owns, pairs = [], []
    for l in range(local):
        own, pair = run(
            functools.partial(weight_kernel, blocks),
            features[l] + grads[l] + [hiddens[l], dpres[l]],
            [((2, units, width), low)] * 2,
        )
        owns.append(own)
        pairs.append(swap(pair, 1))
    expand_grad, reduce_grad = run(
        functools.partial(total_kernel, local), owns + pairs, [(expand_weight.shape, low)] * 2
    )

    def finish(terms_list):
        groups = [[len(terms) for terms in parts] for parts in terms_list]
        outs = run(
            functools.partial(finish_kernel, groups),
            [item for parts in terms_list for terms in parts for item in terms],
            [((len(terms_list) * cap, width), low)] * planes,
        )
        return cross(outs)

    returned = finish(result_terms)
    output, gating_grad = run(
        functools.partial(output_kernel, planes),
        returned + [tokens, cotangent, target, weight, alive],
        [(tokens.shape, low), ((top, toks), jnp.float32)],
    )
    back = [finish([input_terms[l]]) for l in range(local)]
    (tokens_grad,) = run(
        functools.partial(input_kernel, planes, local),
        [back[l][s] for s in range(planes) for l in range(local)]
        + [tokens, cotangent, target, alive],
        [(tokens.shape, low)],
    )
    return (output, tokens_grad, gating_grad.T, expand_grad, reduce_grad)


def solution(mesh):
    rows = P(("dp", "expert"), None)
    weights = P("expert", "dp", None)

    return jax.shard_map(
        body,
        mesh=mesh,
        in_specs=(rows,) * 6 + (weights,) * 2,
        out_specs=(rows,) * 3 + (weights,) * 2,
        check_vma=False,
    )
```

```python
import functools

import jax
import jax.numpy as jnp
from jax import lax
from jax.experimental import pallas as pl
from jax.experimental.pallas import tpu as pltpu
from jax.sharding import PartitionSpec as P

epsilon = 1e-06
root_half = 0.7071067811865476
density_scale = 0.3989422804014327


def dot(left, right, left_dim, right_dim):
    return lax.dot_general(
        left, right, (((left_dim,), (right_dim,)), ((), ())), preferred_element_type=jnp.float32
    )


def normalize(tokens):
    wide = tokens.astype(jnp.float32)
    centred = wide - jnp.mean(wide, axis=1, keepdims=True)
    inv_scale = lax.rsqrt(jnp.mean(centred * centred, axis=1, keepdims=True) + epsilon)
    return centred * inv_scale, inv_scale


def one_hot(target, rows):
    lanes = lax.broadcasted_iota(jnp.int32, (target.shape[0], rows), 1)
    return (target == lanes).astype(jnp.bfloat16)


def to_column(row, same):
    return jnp.sum(jnp.where(same, row, 0.0), axis=1, keepdims=True)


def route_kernel(
    planes, local, me_ref, *refs
):
    outs, sems = refs[6:-7], refs[-1]
    copies = [
        pltpu.make_async_copy(source, held, sems.at[index])
        for index, (source, held) in enumerate(zip(refs[:6], refs[-7:-1]))
    ]
    for copy in copies:
        copy.start()
    gate_ref, ids_ref, seg_ref, keep_ref, tok_ref, cot_ref = refs[-7:-1]
    *small_copies, tok_copy, cot_copy = copies
    for copy in small_copies:
        copy.wait()
    top, toks = ids_ref.shape
    experts = planes * local
    cap = top * toks // experts
    own_features_ref, own_grads_ref, *outs = outs
    others = planes - 1
    feature_refs = [outs[l * others : (l + 1) * others] for l in range(local)]
    grad_refs = outs[local * others : (local + 1) * others]
    target_ref, weight_ref, alive_ref = outs[(local + 1) * others :]
    seg = seg_ref[...]
    spot = lax.broadcasted_iota(jnp.int32, seg.shape, 1).astype(jnp.float32)
    alive_row = jnp.zeros(seg.shape, jnp.float32)
    for image in range(keep_ref.shape[1]):
        start = jnp.sum((seg < image).astype(jnp.float32), axis=1, keepdims=True)
        limit = keep_ref[0:1, image : image + 1].astype(jnp.float32)
        alive_row = jnp.where((seg == image) & (spot - start < limit), 1.0, alive_row)
    row = lax.broadcasted_iota(jnp.int32, (toks, toks), 0)
    col = lax.broadcasted_iota(jnp.int32, (toks, toks), 1)
    same = row == col
    alive = to_column(alive_row, same)
    width = -(-experts // 128) * 128
    lanes = lax.broadcasted_iota(jnp.int32, (toks, width), 1)
    picks = [
        to_column(ids_ref[k : k + 1, :].astype(jnp.float32), same).astype(jnp.int32)
        for k in range(top)
    ]
    chosen = [(pick == lanes).astype(jnp.float32) for pick in picks]
    every = chosen[0]
    for k in range(1, top):
        every = every + chosen[k]
    before = dot((col < row).astype(jnp.bfloat16), every.astype(jnp.bfloat16), 1, 0)
    me = me_ref[0]
    hots = []
    weights = []
    for k in range(top):
        slot = jnp.sum(before * chosen[k], axis=1, keepdims=True).astype(jnp.int32)
        away = jnp.bitwise_xor(lax.div(picks[k], local), me)
        target = (away * local + lax.rem(picks[k], local)) * cap + slot
        weight = to_column(gate_ref[k : k + 1, :] * alive_row, same)
        target_ref[:, k : k + 1] = target
        weight_ref[:, k : k + 1] = weight
        hots.append(one_hot(target, experts * cap))
        weights.append(weight)
    alive_ref[...] = alive
    tok_copy.wait()
    normed, _ = normalize(tok_ref[...])
    low = jnp.where(alive > 0, normed, 0.0).astype(jnp.bfloat16)
    every_hot = hots[0]
    for k in range(1, top):
        every_hot = every_hot + hots[k]
    features = dot(every_hot, low, 0, 0).astype(jnp.bfloat16)
    own_features_ref[...] = features[: local * cap]
    for away in range(1, planes):
        base = away * local * cap
        for l in range(local):
            feature_refs[l][away - 1][...] = features[base + l * cap : base + (l + 1) * cap]
    cot_copy.wait()
    cot = cot_ref[...].astype(jnp.float32)
    scaled = [(cot * weight).astype(jnp.bfloat16) for weight in weights]
    grads = dot(jnp.concatenate(hots, 0), jnp.concatenate(scaled, 0), 0, 0).astype(jnp.bfloat16)
    own_grads_ref[...] = grads[: local * cap]
    for away in range(1, planes):
        base = away * local * cap
        grad_refs[away - 1][...] = grads[base : base + local * cap]


def join_kernel(others, cap, *refs):
    piece_refs, outs = refs[:others], refs[others:]
    for l, out in enumerate(outs):
        for away, ref in enumerate(piece_refs):
            out[away * cap : (away + 1) * cap] = ref[l * cap : (l + 1) * cap]


def add_kernel(*refs):
    total = refs[0][0].astype(jnp.float32)
    for ref in refs[1:-1]:
        total = total + ref[0].astype(jnp.float32)
    refs[-1][0] = total.astype(jnp.bfloat16)


def joined(own_refs, other_refs):
    return jnp.concatenate(
        [ref[...] for pair in zip(own_refs, other_refs) for ref in pair], 0
    )


def forward_kernel(blocks, parts, held, *refs):
    rows = joined(refs[:blocks], refs[blocks : 2 * blocks])
    up_own, up_pair, down_own, down_pair = refs[2 * blocks : 2 * blocks + 4]
    held_refs = refs[2 * blocks + 4 : 2 * blocks + 4 + held]
    hidden_ref, slope_ref, *outs = refs[2 * blocks + 4 + held :]
    up = jnp.concatenate([up_own[0], up_pair[0]], 0)
    pre = dot(rows, up, 1, 1)
    half = 0.5 * (1.0 + lax.erf(pre * root_half))
    hidden = (pre * half).astype(jnp.bfloat16)
    hidden_ref[...] = hidden
    slope_ref[...] = half + pre * jnp.exp(-0.5 * pre * pre) * density_scale
    down = jnp.concatenate([down_own[0], down_pair[0]], 0)
    spread(dot(hidden, down, 1, 0), blocks, parts, held_refs, outs)


def spread(result, blocks, parts, held_refs, outs):
    block_rows = result.shape[0] // blocks
    for held_ref, ref in zip(held_refs, outs):
        ref[:, : held_ref.shape[1]] = held_ref[...]
    for number, (start, stop, slots) in enumerate(parts):
        for index, pair in enumerate(slots):
            for ref, block in zip(outs[2 * number : 2 * number + 2], pair):
                base = block * block_rows
                end = ref.shape[1]
                ref[index, end - (stop - start) : end] = result[
                    base + start : base + stop
                ].astype(jnp.bfloat16)


def backward_kernel(blocks, parts, held, *refs):
    grads = joined(refs[:blocks], refs[blocks : 2 * blocks])
    up_own, up_pair, down_own, down_pair, slope_ref = refs[2 * blocks : 2 * blocks + 5]
    held_refs = refs[2 * blocks + 5 : 2 * blocks + 5 + held]
    dpre_ref, *outs = refs[2 * blocks + 5 + held :]
    down = jnp.concatenate([down_own[0], down_pair[0]], 0)
    dpre = (dot(grads, down, 1, 1) * slope_ref[...]).astype(jnp.bfloat16)
    dpre_ref[...] = dpre
    up = jnp.concatenate([up_own[0], up_pair[0]], 0)
    spread(dot(dpre, up, 1, 0), blocks, parts, held_refs, outs)


def weight_kernel(blocks, *refs):
    rows = joined(refs[:blocks], refs[blocks : 2 * blocks])
    grads = joined(refs[2 * blocks : 3 * blocks], refs[3 * blocks : 4 * blocks])
    hidden_ref, dpre_ref, own_ref, pair_ref = refs[4 * blocks :]
    units = own_ref.shape[1]
    for index, (left_ref, right) in enumerate(((dpre_ref, rows), (hidden_ref, grads))):
        product = dot(left_ref[...], right, 0, 0)
        own_ref[index] = product[:units].astype(jnp.bfloat16)
        pair_ref[index] = product[units:].astype(jnp.bfloat16)


def total_kernel(local, *refs):
    own_refs = refs[:local]
    pair_refs = refs[local : 2 * local]
    out_refs = refs[2 * local :]
    for l in range(local):
        for index, ref in enumerate(out_refs):
            ref[l] = (
                own_refs[l][index].astype(jnp.float32) + pair_refs[l][index].astype(jnp.float32)
            ).astype(jnp.bfloat16)


def summed(refs):
    total = refs[0][0].astype(jnp.float32)
    for ref in refs[1:]:
        total = total + ref[0].astype(jnp.float32)
    return total.astype(jnp.bfloat16)


def finish_kernel(groups, *refs):
    outs = refs[sum(count for counts in groups for count in counts) :]
    cap = outs[0].shape[0] // len(groups)
    used = 0
    for l, counts in enumerate(groups):
        sums = []
        for count in counts:
            sums.append(summed(refs[used : used + count]))
            used += count
        low = jnp.concatenate(sums, 0)
        for index, out in enumerate(outs):
            out[l * cap : (l + 1) * cap] = low[index * cap : (index + 1) * cap]


def output_kernel(count, *refs):
    tok_ref, cot_ref, target_ref, weight_ref, alive_ref, out_ref, gating_ref = refs[-7:]
    results = jnp.concatenate(
        [summed(refs[:count])] + [ref[...] for ref in refs[count:-7]], 0
    )
    toks = tok_ref.shape[0]
    row = lax.broadcasted_iota(jnp.int32, (toks, toks), 0)
    same = row == lax.broadcasted_iota(jnp.int32, (toks, toks), 1)
    total = tok_ref[...].astype(jnp.float32)
    cot = cot_ref[...].astype(jnp.float32)
    for k in range(target_ref.shape[1]):
        picked = dot(one_hot(target_ref[:, k : k + 1], results.shape[0]), results, 1, 0)
        total = total + weight_ref[:, k : k + 1] * picked
        column = alive_ref[...] * jnp.sum(cot * picked, axis=1, keepdims=True)
        gating_ref[k : k + 1, :] = jnp.sum(jnp.where(same, column, 0.0), axis=0, keepdims=True)
    out_ref[...] = total.astype(jnp.bfloat16)


def input_kernel(count, *refs):
    tok_ref, cot_ref, target_ref, alive_ref, out_ref = refs[-5:]
    grads = jnp.concatenate([summed(refs[:count])] + [ref[...] for ref in refs[count:-5]], 0)
    hot = one_hot(target_ref[:, 0:1], grads.shape[0])
    for k in range(1, target_ref.shape[1]):
        hot = hot + one_hot(target_ref[:, k : k + 1], grads.shape[0])
    dnorm = alive_ref[...] * dot(hot, grads, 1, 0)
    normed, inv_scale = normalize(tok_ref[...])
    inner = jnp.mean(dnorm * normed, axis=1, keepdims=True)
    change = dnorm - jnp.mean(dnorm, axis=1, keepdims=True) - normed * inner
    out_ref[...] = (cot_ref[...].astype(jnp.float32) + inv_scale * change).astype(jnp.bfloat16)


def whole(array):
    rank = len(array.shape)
    return pl.BlockSpec(array.shape, lambda *_: (0,) * rank)


def part(array, index):
    rank = len(array.shape)
    return pl.BlockSpec((1,) + array.shape[1:], lambda *_: (index,) + (0,) * (rank - 1))


def slab(array, index, rows):
    return pl.BlockSpec((rows, array.shape[1]), lambda *_: (index, 0))


def spec_of(item):
    if not isinstance(item, tuple):
        return whole(item)
    return part(*item) if len(item) == 2 else slab(*item)


def run(kernel, inputs, outs):
    arrays = [item[0] if isinstance(item, tuple) else item for item in inputs]
    specs = [spec_of(item) for item in inputs]
    outs = [jax.ShapeDtypeStruct(shape, dtype) for shape, dtype in outs]
    return pl.pallas_call(
        kernel,
        out_shape=outs,
        grid=(1,),
        in_specs=specs,
        out_specs=[whole(out) for out in outs],
        compiler_params=pltpu.CompilerParams(vmem_limit_bytes=40 << 20),
    )(*arrays)


def body(
    tokens, cotangent, gate_weights, expert_ids, segments, keep_counts, expand_weight, reduce_weight
):
    toks, width = tokens.shape
    top = expert_ids.shape[1]
    groups = lax.axis_size("dp")
    planes = lax.axis_size("expert")
    local, units, _ = expand_weight.shape
    cap = top * toks // (planes * local)
    blocks = groups // 2
    bits = [1 << bit for bit in range(1, groups.bit_length() - 1)]
    block_rows = planes * cap
    low = jnp.bfloat16

    def swap(values, mask):
        return lax.ppermute(values, "dp", [(i, i ^ mask) for i in range(groups)])

    def cross(pieces):
        away = []
        for s, piece in enumerate(pieces, 1):
            away.append(lax.ppermute(piece, "expert", [(i, i ^ s) for i in range(planes)]))
        return away

    def order_of(index):
        shift = index % len(bits)
        return bits[shift:] + bits[:shift]

    def gather(own, order):
        held = {0: own}
        for bit in order:
            for block in sorted(held):
                held[block | bit] = swap(held[block], bit)
        return [held[2 * index] for index in range(blocks)]

    def part_of(start, stop, order):
        bit = order[0] // 2
        slots = tuple((block | bit, block) for block in range(blocks) if not block & bit)
        return start, stop, slots

    def scatter(send, keep, order):
        bit = order[0]
        arrived = swap(send, bit)
        terms = {
            2 * slots[1]: [(keep, index), (arrived, index)]
            for index, slots in enumerate(part_of(0, 0, order)[2])
        }
        for bit in order[1:]:
            leaving = [block for block in sorted(terms) if block & bit]
            sums = [
                run(add_kernel, terms[block], [((1,) + send.shape[1:], low)])[0]
                for block in leaving
            ]
            sums = sums[0] if len(sums) == 1 else jnp.concatenate(sums, 0)
            arrived = swap(sums, bit)
            for index, block in enumerate(leaving):
                terms[block ^ bit].append((arrived, index))
                del terms[block]
        return terms[0]

    me = lax.axis_index("expert").astype(jnp.int32).reshape(1)
    others = planes - 1
    sources = [gate_weights.T, expert_ids.T, segments, keep_counts, tokens, cotangent]
    routed = pl.pallas_call(
        functools.partial(route_kernel, planes, local),
        out_shape=[jax.ShapeDtypeStruct((local * cap, width), low)] * 2
        + [jax.ShapeDtypeStruct((cap, width), low)] * (local * others)
        + [jax.ShapeDtypeStruct((local * cap, width), low)] * others
        + [
            jax.ShapeDtypeStruct((toks, top), jnp.int32),
            jax.ShapeDtypeStruct((toks, top), jnp.float32),
            jax.ShapeDtypeStruct((toks, 1), jnp.float32),
        ],
        in_specs=[pl.BlockSpec(memory_space=pltpu.SMEM)]
        + [pl.BlockSpec(memory_space=pltpu.HBM)] * len(sources),
        scratch_shapes=[pltpu.VMEM(source.shape, source.dtype) for source in sources]
        + [pltpu.SemaphoreType.DMA((len(sources),))],
        compiler_params=pltpu.CompilerParams(vmem_limit_bytes=40 << 20),
        name="route",
    )(me, *sources)
    own_features, own_grads, *away = routed[:-3]
    target, weight, alive = routed[-3:]
    up_pair = swap(expand_weight, 1)
    down_pair = swap(reduce_weight, 1)

    near_features = gather(own_features, order_of(0))
    near_grads = gather(own_grads, order_of(1))
    features = []
    for l in range(local):
        pieces = cross(away[l * others : (l + 1) * others])
        (own,) = run(
            functools.partial(join_kernel, others, cap), pieces, [((others * cap, width), low)]
        )
        near = [(block, l, cap) for block in near_features]
        features.append(near + gather(own, order_of(l)))
    pieces = cross(away[local * others :])
    owns = run(
        functools.partial(join_kernel, others, cap), pieces, [((others * cap, width), low)] * local
    )
    grads = [
        [(block, l, cap) for block in near_grads] + gather(owns[l], order_of(l))
        for l in range(local)
    ]

    rows = blocks * block_rows
    flat = ((rows, 2 * units), low)
    wide = ((rows, 2 * units), jnp.float32)

    def outs_of(l, parts):
        sizes = [(l + 1) * cap] + [stop - start for start, stop, _ in parts[1:]]
        return [((blocks // 2, size, width), low) for size in sizes for _ in range(2)]

    hiddens, slopes, result_terms, held = [], [], [], []
    for l in range(local):
        parts = [part_of(0, cap, order_of(1)), part_of(cap, block_rows, order_of(l))]
        hidden, slope, *sends = run(
            functools.partial(forward_kernel, blocks, parts, len(held)),
            features[l]
            + [(expand_weight, l), (up_pair, l), (reduce_weight, l), (down_pair, l)]
            + held,
            [flat, wide] + outs_of(l, parts),
        )
        hiddens.append(hidden)
        slopes.append(slope)
        held = sends[:2]
        result_terms.append([scatter(sends[2], sends[3], order_of(l))])
    near_results = scatter(*held, order_of(1))
    half = cap + others * cap // 32 * 16
    dpres, input_terms, held = [], [], []
    for l in range(local):
        parts = [
            part_of(0, cap, order_of(0)),
            part_of(cap, half, order_of(0)),
            part_of(half, block_rows, order_of(1)),
        ]
        dpre, *sends = run(
            functools.partial(backward_kernel, blocks, parts, len(held)),
            grads[l]
            + [(expand_weight, l), (up_pair, l), (reduce_weight, l), (down_pair, l), slopes[l]]
            + held,
            [flat] + outs_of(l, parts),
        )
        dpres.append(dpre)
        held = sends[:2]
        input_terms.append(
            [scatter(*sends[2 * index + 2 : 2 * index + 4], order_of(index)) for index in range(2)]
        )
    near_inputs = scatter(*held, order_of(0))
    owns, pairs = [], []
    for l in range(local):
        own, pair = run(
            functools.partial(weight_kernel, blocks),
            features[l] + grads[l] + [hiddens[l], dpres[l]],
            [((2, units, width), low)] * 2,
        )
        owns.append(own)
        pairs.append(swap(pair, 1))
    expand_grad, reduce_grad = run(
        functools.partial(total_kernel, local), owns + pairs, [(expand_weight.shape, low)] * 2
    )

    def finish(terms_list):
        groups = [[len(terms) for terms in parts] for parts in terms_list]
        outs = run(
            functools.partial(finish_kernel, groups),
            [item for parts in terms_list for terms in parts for item in terms],
            [((len(terms_list) * cap, width), low)] * others,
        )
        return cross(outs)

    returned = finish(result_terms)
    output, gating_grad = run(
        functools.partial(output_kernel, len(near_results)),
        near_results + returned + [tokens, cotangent, target, weight, alive],
        [(tokens.shape, low), ((top, toks), jnp.float32)],
    )
    back = [finish([input_terms[l]]) for l in range(local)]
    (tokens_grad,) = run(
        functools.partial(input_kernel, len(near_inputs)),
        near_inputs
        + [back[l][s] for s in range(others) for l in range(local)]
        + [tokens, cotangent, target, alive],
        [(tokens.shape, low)],
    )
    return (output, tokens_grad, gating_grad.T, expand_grad, reduce_grad)


def solution(mesh):
    rows = P(("dp", "expert"), None)
    weights = P("expert", "dp", None)

    return jax.shard_map(
        body,
        mesh=mesh,
        in_specs=(rows,) * 6 + (weights,) * 2,
        out_specs=(rows,) * 3 + (weights,) * 2,
        check_vma=False,
    )
```

```python
import functools

import jax
import jax.numpy as jnp
from jax import lax
from jax.experimental import pallas as pl
from jax.experimental.pallas import tpu as pltpu
from jax.sharding import PartitionSpec as P

epsilon = 1e-06
root_half = 0.7071067811865476
density_scale = 0.3989422804014327

split_inputs = False
split_results = False
split_grads = False
merge_near = False
merge_features = False
merge_grads = False
turns = {
    "d0": 0,
    "d1": 1,
    "g0": 0,
    "g1": 1,
    "pd": 0,
    "pg": 1,
    "px": 0,
    "py": 1,
    "x0": 0,
    "x1": 1,
    "y0": 0,
    "y1": 1,
}


def dot(left, right, left_dim, right_dim):
    return lax.dot_general(
        left, right, (((left_dim,), (right_dim,)), ((), ())), preferred_element_type=jnp.float32
    )


def normalize(tokens):
    wide = tokens.astype(jnp.float32)
    centred = wide - jnp.mean(wide, axis=1, keepdims=True)
    inv_scale = lax.rsqrt(jnp.mean(centred * centred, axis=1, keepdims=True) + epsilon)
    return centred * inv_scale, inv_scale


def one_hot(target, rows):
    lanes = lax.broadcasted_iota(jnp.int32, (target.shape[0], rows), 1)
    return (target == lanes).astype(jnp.bfloat16)


def to_column(row, same):
    return jnp.sum(jnp.where(same, row, 0.0), axis=1, keepdims=True)


def scatter_far(refs, values, others, near):
    for number, ref in enumerate(refs):
        index, away = number // others, number % others
        rows = ref.shape[0]
        base = (away + 1) * near + index * rows
        ref[...] = values[base : base + rows]


def route_kernel(
    planes, local, me_ref, *refs
):
    outs, sems = refs[6:-7], refs[-1]
    copies = [
        pltpu.make_async_copy(source, held, sems.at[index])
        for index, (source, held) in enumerate(zip(refs[:6], refs[-7:-1]))
    ]
    for copy in copies:
        copy.start()
    gate_ref, ids_ref, seg_ref, keep_ref, tok_ref, cot_ref = refs[-7:-1]
    *small_copies, tok_copy, cot_copy = copies
    for copy in small_copies:
        copy.wait()
    top, toks = ids_ref.shape
    experts = planes * local
    cap = top * toks // experts
    near_refs = outs[: 1 if merge_near else 2]
    others = planes - 1
    feature_parts = 1 if merge_features else local
    far_refs = outs[len(near_refs) : -3]
    feature_refs, grad_refs = far_refs[: feature_parts * others], far_refs[feature_parts * others :]
    target_ref, weight_ref, alive_ref = outs[-3:]
    seg = seg_ref[...]
    spot = lax.broadcasted_iota(jnp.int32, seg.shape, 1).astype(jnp.float32)
    alive_row = jnp.zeros(seg.shape, jnp.float32)
    for image in range(keep_ref.shape[1]):
        start = jnp.sum((seg < image).astype(jnp.float32), axis=1, keepdims=True)
        limit = keep_ref[0:1, image : image + 1].astype(jnp.float32)
        alive_row = jnp.where((seg == image) & (spot - start < limit), 1.0, alive_row)
    row = lax.broadcasted_iota(jnp.int32, (toks, toks), 0)
    col = lax.broadcasted_iota(jnp.int32, (toks, toks), 1)
    same = row == col
    alive = to_column(alive_row, same)
    width = -(-experts // 128) * 128
    lanes = lax.broadcasted_iota(jnp.int32, (toks, width), 1)
    picks = [
        to_column(ids_ref[k : k + 1, :].astype(jnp.float32), same).astype(jnp.int32)
        for k in range(top)
    ]
    chosen = [(pick == lanes).astype(jnp.float32) for pick in picks]
    every = chosen[0]
    for k in range(1, top):
        every = every + chosen[k]
    before = dot((col < row).astype(jnp.bfloat16), every.astype(jnp.bfloat16), 1, 0)
    me = me_ref[0]
    hots = []
    weights = []
    for k in range(top):
        slot = jnp.sum(before * chosen[k], axis=1, keepdims=True).astype(jnp.int32)
        away = jnp.bitwise_xor(lax.div(picks[k], local), me)
        target = (away * local + lax.rem(picks[k], local)) * cap + slot
        weight = to_column(gate_ref[k : k + 1, :] * alive_row, same)
        target_ref[:, k : k + 1] = target
        weight_ref[:, k : k + 1] = weight
        hots.append(one_hot(target, experts * cap))
        weights.append(weight)
    alive_ref[...] = alive
    tok_copy.wait()
    normed, _ = normalize(tok_ref[...])
    low = jnp.where(alive > 0, normed, 0.0).astype(jnp.bfloat16)
    every_hot = hots[0]
    for k in range(1, top):
        every_hot = every_hot + hots[k]
    features = dot(every_hot, low, 0, 0).astype(jnp.bfloat16)
    near = local * cap
    near_refs[0][:near] = features[:near]
    scatter_far(feature_refs, features, others, near)
    cot_copy.wait()
    cot = cot_ref[...].astype(jnp.float32)
    scaled = [(cot * weight).astype(jnp.bfloat16) for weight in weights]
    grads = dot(jnp.concatenate(hots, 0), jnp.concatenate(scaled, 0), 0, 0).astype(jnp.bfloat16)
    near_refs[-1][near_refs[-1].shape[0] - near :] = grads[:near]
    scatter_far(grad_refs, grads, others, near)


def join_kernel(others, cap, merge, *refs):
    piece_refs, outs = refs[:others], refs[others:]
    for l in range(piece_refs[0].shape[0] // cap):
        out = outs[0 if merge else l]
        base = l * others * cap if merge else 0
        for away, ref in enumerate(piece_refs):
            out[base + away * cap : base + (away + 1) * cap] = ref[l * cap : (l + 1) * cap]


def add_kernel(*refs):
    total = refs[0][0].astype(jnp.float32)
    for ref in refs[1:-1]:
        total = total + ref[0].astype(jnp.float32)
    refs[-1][0] = total.astype(jnp.bfloat16)


def joined(own_refs, other_refs):
    return jnp.concatenate(
        [ref[...] for pair in zip(own_refs, other_refs) for ref in pair], 0
    )


def forward_kernel(blocks, parts, held, *refs):
    rows = joined(refs[:blocks], refs[blocks : 2 * blocks])
    up_own, up_pair, down_own, down_pair = refs[2 * blocks : 2 * blocks + 4]
    held_refs = refs[2 * blocks + 4 : 2 * blocks + 4 + held]
    hidden_ref, slope_ref, *outs = refs[2 * blocks + 4 + held :]
    up = jnp.concatenate([up_own[0], up_pair[0]], 0)
    pre = dot(rows, up, 1, 1)
    half = 0.5 * (1.0 + lax.erf(pre * root_half))
    hidden = (pre * half).astype(jnp.bfloat16)
    hidden_ref[...] = hidden
    slope_ref[...] = half + pre * jnp.exp(-0.5 * pre * pre) * density_scale
    down = jnp.concatenate([down_own[0], down_pair[0]], 0)
    spread(dot(hidden, down, 1, 0), blocks, parts, held_refs, outs)


def spread(result, blocks, parts, held_refs, outs):
    block_rows = result.shape[0] // blocks
    for held_ref, ref in zip(held_refs, outs):
        ref[:, : held_ref.shape[1]] = held_ref[...]
    for number, (start, stop, slots) in enumerate(parts):
        for index, pair in enumerate(slots):
            for ref, block in zip(outs[2 * number : 2 * number + 2], pair):
                base = block * block_rows
                end = ref.shape[1]
                ref[index, end - (stop - start) : end] = result[
                    base + start : base + stop
                ].astype(jnp.bfloat16)


def backward_kernel(blocks, parts, held, *refs):
    grads = joined(refs[:blocks], refs[blocks : 2 * blocks])
    up_own, up_pair, down_own, down_pair, slope_ref = refs[2 * blocks : 2 * blocks + 5]
    held_refs = refs[2 * blocks + 5 : 2 * blocks + 5 + held]
    dpre_ref, *outs = refs[2 * blocks + 5 + held :]
    down = jnp.concatenate([down_own[0], down_pair[0]], 0)
    dpre = (dot(grads, down, 1, 1) * slope_ref[...]).astype(jnp.bfloat16)
    dpre_ref[...] = dpre
    up = jnp.concatenate([up_own[0], up_pair[0]], 0)
    spread(dot(dpre, up, 1, 0), blocks, parts, held_refs, outs)


def weight_kernel(blocks, *refs):
    rows = joined(refs[:blocks], refs[blocks : 2 * blocks])
    grads = joined(refs[2 * blocks : 3 * blocks], refs[3 * blocks : 4 * blocks])
    hidden_ref, dpre_ref, own_ref, pair_ref = refs[4 * blocks :]
    units = own_ref.shape[1]
    for index, (left_ref, right) in enumerate(((dpre_ref, rows), (hidden_ref, grads))):
        product = dot(left_ref[...], right, 0, 0)
        own_ref[index] = product[:units].astype(jnp.bfloat16)
        pair_ref[index] = product[units:].astype(jnp.bfloat16)


def total_kernel(local, *refs):
    own_refs = refs[:local]
    pair_refs = refs[local : 2 * local]
    out_refs = refs[2 * local :]
    for l in range(local):
        for index, ref in enumerate(out_refs):
            ref[l] = (
                own_refs[l][index].astype(jnp.float32) + pair_refs[l][index].astype(jnp.float32)
            ).astype(jnp.bfloat16)


def summed(refs):
    total = refs[0][0].astype(jnp.float32)
    for ref in refs[1:]:
        total = total + ref[0].astype(jnp.float32)
    return total.astype(jnp.bfloat16)


def finish_kernel(groups, *refs):
    outs = refs[sum(count for counts in groups for count in counts) :]
    cap = outs[0].shape[0] // len(groups)
    used = 0
    for l, counts in enumerate(groups):
        sums = []
        for count in counts:
            sums.append(summed(refs[used : used + count]))
            used += count
        low = jnp.concatenate(sums, 0)
        for index, out in enumerate(outs):
            out[l * cap : (l + 1) * cap] = low[index * cap : (index + 1) * cap]


def output_kernel(count, *refs):
    tok_ref, cot_ref, target_ref, weight_ref, alive_ref, out_ref, gating_ref = refs[-7:]
    results = jnp.concatenate(
        [summed(refs[:count])] + [ref[...] for ref in refs[count:-7]], 0
    )
    toks = tok_ref.shape[0]
    row = lax.broadcasted_iota(jnp.int32, (toks, toks), 0)
    same = row == lax.broadcasted_iota(jnp.int32, (toks, toks), 1)
    total = tok_ref[...].astype(jnp.float32)
    cot = cot_ref[...].astype(jnp.float32)
    for k in range(target_ref.shape[1]):
        picked = dot(one_hot(target_ref[:, k : k + 1], results.shape[0]), results, 1, 0)
        total = total + weight_ref[:, k : k + 1] * picked
        column = alive_ref[...] * jnp.sum(cot * picked, axis=1, keepdims=True)
        gating_ref[k : k + 1, :] = jnp.sum(jnp.where(same, column, 0.0), axis=0, keepdims=True)
    out_ref[...] = total.astype(jnp.bfloat16)


def input_kernel(count, *refs):
    tok_ref, cot_ref, target_ref, alive_ref, out_ref = refs[-5:]
    grads = jnp.concatenate([summed(refs[:count])] + [ref[...] for ref in refs[count:-5]], 0)
    hot = one_hot(target_ref[:, 0:1], grads.shape[0])
    for k in range(1, target_ref.shape[1]):
        hot = hot + one_hot(target_ref[:, k : k + 1], grads.shape[0])
    dnorm = alive_ref[...] * dot(hot, grads, 1, 0)
    normed, inv_scale = normalize(tok_ref[...])
    inner = jnp.mean(dnorm * normed, axis=1, keepdims=True)
    change = dnorm - jnp.mean(dnorm, axis=1, keepdims=True) - normed * inner
    out_ref[...] = (cot_ref[...].astype(jnp.float32) + inv_scale * change).astype(jnp.bfloat16)


def whole(array):
    rank = len(array.shape)
    return pl.BlockSpec(array.shape, lambda *_: (0,) * rank)


def part(array, index):
    rank = len(array.shape)
    return pl.BlockSpec((1,) + array.shape[1:], lambda *_: (index,) + (0,) * (rank - 1))


def slab(array, index, rows):
    return pl.BlockSpec((rows, array.shape[1]), lambda *_: (index, 0))


def spec_of(item):
    if not isinstance(item, tuple):
        return whole(item)
    return part(*item) if len(item) == 2 else slab(*item)


def run(kernel, inputs, outs):
    arrays = [item[0] if isinstance(item, tuple) else item for item in inputs]
    specs = [spec_of(item) for item in inputs]
    outs = [jax.ShapeDtypeStruct(shape, dtype) for shape, dtype in outs]
    return pl.pallas_call(
        kernel,
        out_shape=outs,
        grid=(1,),
        in_specs=specs,
        out_specs=[whole(out) for out in outs],
        compiler_params=pltpu.CompilerParams(vmem_limit_bytes=24 << 20),
    )(*arrays)


def body(
    tokens, cotangent, gate_weights, expert_ids, segments, keep_counts, expand_weight, reduce_weight
):
    toks, width = tokens.shape
    top = expert_ids.shape[1]
    groups = lax.axis_size("dp")
    planes = lax.axis_size("expert")
    local, units, _ = expand_weight.shape
    cap = top * toks // (planes * local)
    blocks = groups // 2
    bits = [1 << bit for bit in range(1, groups.bit_length() - 1)]
    block_rows = planes * cap
    low = jnp.bfloat16

    def swap(values, mask):
        return lax.ppermute(values, "dp", [(i, i ^ mask) for i in range(groups)])

    def cross(pieces):
        away = []
        for s, piece in enumerate(pieces, 1):
            away.append(lax.ppermute(piece, "expert", [(i, i ^ s) for i in range(planes)]))
        return away

    def order_of(name):
        shift = turns[name] % len(bits)
        return bits[shift:] + bits[:shift]

    def gather(name, own):
        held = {0: own}
        for bit in order_of(name):
            for block in sorted(held):
                held[block | bit] = swap(held[block], bit)
        return [held[2 * index] for index in range(blocks)]

    def part_of(name, start, stop):
        bit = order_of(name)[0] // 2
        slots = tuple((block | bit, block) for block in range(blocks) if not block & bit)
        return start, stop, slots

    def scatter(name, send, keep):
        order = order_of(name)
        bit = order[0]
        arrived = swap(send, bit)
        terms = {
            2 * slots[1]: [(keep, index), (arrived, index)]
            for index, slots in enumerate(part_of(name, 0, 0)[2])
        }
        for bit in order[1:]:
            leaving = [block for block in sorted(terms) if block & bit]
            sums = [
                run(add_kernel, terms[block], [((1,) + send.shape[1:], low)])[0]
                for block in leaving
            ]
            sums = sums[0] if len(sums) == 1 else jnp.concatenate(sums, 0)
            arrived = swap(sums, bit)
            for index, block in enumerate(leaving):
                terms[block ^ bit].append((arrived, index))
                del terms[block]
        return terms[0]

    me = lax.axis_index("expert").astype(jnp.int32).reshape(1)
    others = planes - 1
    near_parts = 1 if merge_near else 2
    feature_parts = 1 if merge_features else local
    grad_parts = local if split_grads else 1
    sources = [gate_weights.T, expert_ids.T, segments, keep_counts, tokens, cotangent]
    routed = pl.pallas_call(
        functools.partial(route_kernel, planes, local),
        out_shape=[jax.ShapeDtypeStruct((2 * local * cap // near_parts, width), low)] * near_parts
        + [jax.ShapeDtypeStruct((local * cap // feature_parts, width), low)]
        * (feature_parts * others)
        + [jax.ShapeDtypeStruct((local * cap // grad_parts, width), low)] * (grad_parts * others)
        + [
            jax.ShapeDtypeStruct((toks, top), jnp.int32),
            jax.ShapeDtypeStruct((toks, top), jnp.float32),
            jax.ShapeDtypeStruct((toks, 1), jnp.float32),
        ],
        in_specs=[pl.BlockSpec(memory_space=pltpu.SMEM)]
        + [pl.BlockSpec(memory_space=pltpu.HBM)] * len(sources),
        scratch_shapes=[pltpu.VMEM(source.shape, source.dtype) for source in sources]
        + [pltpu.SemaphoreType.DMA((len(sources),))],
        compiler_params=pltpu.CompilerParams(vmem_limit_bytes=24 << 20),
        name="route",
    )(me, *[pltpu.with_memory_space_constraint(source, pltpu.HBM) for source in sources])
    away = routed[near_parts:-3]
    target, weight, alive = routed[-3:]
    up_pair = swap(expand_weight, 1)
    down_pair = swap(reduce_weight, 1)

    far = others * cap
    if merge_near:
        near = gather("px", routed[0])
        near_features = [[(block, l, cap) for block in near] for l in range(local)]
        near_grads = [[(block, local + l, cap) for block in near] for l in range(local)]
    else:
        near_blocks = gather("px", routed[0]), gather("pg", routed[1])
        near_features, near_grads = [
            [[(block, l, cap) for block in held] for l in range(local)] for held in near_blocks
        ]

    def collect(name, pieces, split, merge):
        count = local if split else 1
        owns = []
        for index in range(count):
            arrived = cross(pieces[index * others : (index + 1) * others])
            owns += run(
                functools.partial(join_kernel, others, cap, merge),
                arrived,
                [((local * far if merge else far, width), low)]
                * (1 if merge else local // count),
            )
        if merge:
            held = gather(name, owns[0])
            return [[(block, l, far) for block in held] for l in range(local)]
        return [gather(f"{name}{l}", owns[l]) for l in range(local)]

    features = collect("x", away[: feature_parts * others], not merge_features, merge_features)
    features = [near_features[l] + features[l] for l in range(local)]
    grads = collect("g", away[feature_parts * others :], split_grads, merge_grads)
    grads = [near_grads[l] + grads[l] for l in range(local)]

    rows = blocks * block_rows
    flat = ((rows, 2 * units), low)
    wide = ((rows, 2 * units), jnp.float32)

    def outs_of(l, parts):
        sizes = [(l + 1) * cap] + [stop - start for start, stop, _ in parts[1:]]
        return [((blocks // 2, size, width), low) for size in sizes for _ in range(2)]

    hiddens, slopes, result_terms, held = [], [], [], []
    for l in range(local):
        parts = [part_of("py", 0, cap), part_of(f"y{l}", cap, block_rows)]
        hidden, slope, *sends = run(
            functools.partial(forward_kernel, blocks, parts, len(held)),
            features[l]
            + [(expand_weight, l), (up_pair, l), (reduce_weight, l), (down_pair, l)]
            + held,
            [flat, wide] + outs_of(l, parts),
        )
        hiddens.append(hidden)
        slopes.append(slope)
        held = sends[:2]
        result_terms.append([scatter(f"y{l}", sends[2], sends[3])])
    near_results = scatter("py", *held)
    dpres, input_terms, held = [], [], []
    for l in range(local):
        parts = [part_of("pd", 0, cap)]
        if split_inputs:
            half = cap + others * cap // 32 * 16
            named = [(f"d{l}0", cap, half), (f"d{l}1", half, block_rows)]
        else:
            named = [(f"d{l}", cap, block_rows)]
        parts += [part_of(*item) for item in named]
        dpre, *sends = run(
            functools.partial(backward_kernel, blocks, parts, len(held)),
            grads[l]
            + [(expand_weight, l), (up_pair, l), (reduce_weight, l), (down_pair, l), slopes[l]]
            + held,
            [flat] + outs_of(l, parts),
        )
        dpres.append(dpre)
        held = sends[:2]
        input_terms.append(
            [
                scatter(item[0], *sends[2 * index + 2 : 2 * index + 4])
                for index, item in enumerate(named)
            ]
        )
    near_inputs = scatter("pd", *held)
    owns, pairs = [], []
    for l in range(local):
        own, pair = run(
            functools.partial(weight_kernel, blocks),
            features[l] + grads[l] + [hiddens[l], dpres[l]],
            [((2, units, width), low)] * 2,
        )
        owns.append(own)
        pairs.append(swap(pair, 1))
    expand_grad, reduce_grad = run(
        functools.partial(total_kernel, local), owns + pairs, [(expand_weight.shape, low)] * 2
    )

    def finish(terms_list):
        groups = [[len(terms) for terms in parts] for parts in terms_list]
        outs = run(
            functools.partial(finish_kernel, groups),
            [item for parts in terms_list for terms in parts for item in terms],
            [((len(terms_list) * cap, width), low)] * others,
        )
        return cross(outs)

    if split_results:
        returned = [finish([result_terms[l]]) for l in range(local)]
        returned = [returned[l][s] for s in range(others) for l in range(local)]
    else:
        returned = finish(result_terms)
    output, gating_grad = run(
        functools.partial(output_kernel, len(near_results)),
        near_results + returned + [tokens, cotangent, target, weight, alive],
        [(tokens.shape, low), ((top, toks), jnp.float32)],
    )
    back = [finish([input_terms[l]]) for l in range(local)]
    (tokens_grad,) = run(
        functools.partial(input_kernel, len(near_inputs)),
        near_inputs
        + [back[l][s] for s in range(others) for l in range(local)]
        + [tokens, cotangent, target, alive],
        [(tokens.shape, low)],
    )
    return (output, tokens_grad, gating_grad.T, expand_grad, reduce_grad)


def solution(mesh):
    rows = P(("dp", "expert"), None)
    weights = P("expert", "dp", None)

    return jax.shard_map(
        body,
        mesh=mesh,
        in_specs=(rows,) * 6 + (weights,) * 2,
        out_specs=(rows,) * 3 + (weights,) * 2,
        check_vma=False,
    )
```

```python
import functools

import jax
import jax.numpy as jnp
from jax import lax
from jax.experimental import pallas as pl
from jax.experimental.pallas import tpu as pltpu
from jax.sharding import PartitionSpec as P

epsilon = 1e-06
root_half = 0.7071067811865476
density_scale = 0.3989422804014327

split_inputs = False
split_results = False
split_grads = False
merge_near = False
merge_features = False
merge_grads = False
turns = {
    "d0": 0,
    "d1": 1,
    "g0": 0,
    "g1": 1,
    "pd": 0,
    "pg": 1,
    "px": 0,
    "py": 1,
    "x0": 0,
    "x1": 1,
    "y0": 0,
    "y1": 1,
}


def dot(left, right, left_dim, right_dim):
    return lax.dot_general(
        left, right, (((left_dim,), (right_dim,)), ((), ())), preferred_element_type=jnp.float32
    )


def normalize(tokens):
    wide = tokens.astype(jnp.float32)
    centred = wide - jnp.mean(wide, axis=1, keepdims=True)
    inv_scale = lax.rsqrt(jnp.mean(centred * centred, axis=1, keepdims=True) + epsilon)
    return centred * inv_scale, inv_scale


def one_hot(target, rows):
    lanes = lax.broadcasted_iota(jnp.int32, (target.shape[0], rows), 1)
    return (target == lanes).astype(jnp.bfloat16)


def to_column(row, same):
    return jnp.sum(jnp.where(same, row, 0.0), axis=1, keepdims=True)


def scatter_far(refs, values, others, near):
    for number, ref in enumerate(refs):
        index, away = number // others, number % others
        rows = ref.shape[0]
        base = (away + 1) * near + index * rows
        ref[...] = values[base : base + rows]


def route_kernel(
    planes, local, me_ref, *refs
):
    outs, sems = refs[6:-7], refs[-1]
    copies = [
        pltpu.make_async_copy(source, held, sems.at[index])
        for index, (source, held) in enumerate(zip(refs[:6], refs[-7:-1]))
    ]
    for copy in copies:
        copy.start()
    gate_ref, ids_ref, seg_ref, keep_ref, tok_ref, cot_ref = refs[-7:-1]
    *small_copies, tok_copy, cot_copy = copies
    for copy in small_copies:
        copy.wait()
    top, toks = ids_ref.shape
    experts = planes * local
    cap = top * toks // experts
    near_refs = outs[: 1 if merge_near else 2]
    others = planes - 1
    feature_parts = 1 if merge_features else local
    far_refs = outs[len(near_refs) : -3]
    feature_refs, grad_refs = far_refs[: feature_parts * others], far_refs[feature_parts * others :]
    target_ref, weight_ref, alive_ref = outs[-3:]
    seg = seg_ref[...]
    spot = lax.broadcasted_iota(jnp.int32, seg.shape, 1).astype(jnp.float32)
    alive_row = jnp.zeros(seg.shape, jnp.float32)
    for image in range(keep_ref.shape[1]):
        start = jnp.sum((seg < image).astype(jnp.float32), axis=1, keepdims=True)
        limit = keep_ref[0:1, image : image + 1].astype(jnp.float32)
        alive_row = jnp.where((seg == image) & (spot - start < limit), 1.0, alive_row)
    row = lax.broadcasted_iota(jnp.int32, (toks, toks), 0)
    col = lax.broadcasted_iota(jnp.int32, (toks, toks), 1)
    same = row == col
    alive = to_column(alive_row, same)
    width = -(-experts // 128) * 128
    lanes = lax.broadcasted_iota(jnp.int32, (toks, width), 1)
    picks = [
        to_column(ids_ref[k : k + 1, :].astype(jnp.float32), same).astype(jnp.int32)
        for k in range(top)
    ]
    chosen = [(pick == lanes).astype(jnp.float32) for pick in picks]
    every = chosen[0]
    for k in range(1, top):
        every = every + chosen[k]
    before = dot((col < row).astype(jnp.bfloat16), every.astype(jnp.bfloat16), 1, 0)
    me = me_ref[0]
    hots = []
    weights = []
    for k in range(top):
        slot = jnp.sum(before * chosen[k], axis=1, keepdims=True).astype(jnp.int32)
        away = jnp.bitwise_xor(lax.div(picks[k], local), me)
        target = (away * local + lax.rem(picks[k], local)) * cap + slot
        weight = to_column(gate_ref[k : k + 1, :] * alive_row, same)
        target_ref[:, k : k + 1] = target
        weight_ref[:, k : k + 1] = weight
        hots.append(one_hot(target, experts * cap))
        weights.append(weight)
    alive_ref[...] = alive
    tok_copy.wait()
    normed, _ = normalize(tok_ref[...])
    low = jnp.where(alive > 0, normed, 0.0).astype(jnp.bfloat16)
    every_hot = hots[0]
    for k in range(1, top):
        every_hot = every_hot + hots[k]
    features = dot(every_hot, low, 0, 0).astype(jnp.bfloat16)
    near = local * cap
    near_refs[0][:near] = features[:near]
    scatter_far(feature_refs, features, others, near)
    cot_copy.wait()
    cot = cot_ref[...].astype(jnp.float32)
    scaled = [(cot * weight).astype(jnp.bfloat16) for weight in weights]
    grads = dot(jnp.concatenate(hots, 0), jnp.concatenate(scaled, 0), 0, 0).astype(jnp.bfloat16)
    near_refs[-1][near_refs[-1].shape[0] - near :] = grads[:near]
    scatter_far(grad_refs, grads, others, near)


def join_kernel(others, cap, merge, *refs):
    piece_refs, outs = refs[:others], refs[others:]
    for l in range(piece_refs[0].shape[0] // cap):
        out = outs[0 if merge else l]
        base = l * others * cap if merge else 0
        for away, ref in enumerate(piece_refs):
            out[base + away * cap : base + (away + 1) * cap] = ref[l * cap : (l + 1) * cap]


def add_kernel(*refs):
    total = refs[0][0].astype(jnp.float32)
    for ref in refs[1:-1]:
        total = total + ref[0].astype(jnp.float32)
    refs[-1][0] = total.astype(jnp.bfloat16)


def joined(own_refs, other_refs):
    return jnp.concatenate(
        [ref[...] for pair in zip(own_refs, other_refs) for ref in pair], 0
    )


def forward_kernel(blocks, parts, held, *refs):
    rows = joined(refs[:blocks], refs[blocks : 2 * blocks])
    up_own, up_pair, down_own, down_pair = refs[2 * blocks : 2 * blocks + 4]
    held_refs = refs[2 * blocks + 4 : 2 * blocks + 4 + held]
    hidden_ref, slope_ref, *outs = refs[2 * blocks + 4 + held :]
    up = jnp.concatenate([up_own[0], up_pair[0]], 0)
    pre = dot(rows, up, 1, 1)
    half = 0.5 * (1.0 + lax.erf(pre * root_half))
    hidden = (pre * half).astype(jnp.bfloat16)
    hidden_ref[...] = hidden
    slope = half + pre * jnp.exp(-0.5 * pre * pre) * density_scale
    slope_ref[...] = slope.astype(slope_ref.dtype)
    down = jnp.concatenate([down_own[0], down_pair[0]], 0)
    spread(dot(hidden, down, 1, 0), blocks, parts, held_refs, outs)


def spread(result, blocks, parts, held_refs, outs):
    block_rows = result.shape[0] // blocks
    for held_ref, ref in zip(held_refs, outs):
        ref[:, : held_ref.shape[1]] = held_ref[...]
    for number, (start, stop, slots) in enumerate(parts):
        for index, pair in enumerate(slots):
            for ref, block in zip(outs[2 * number : 2 * number + 2], pair):
                base = block * block_rows
                end = ref.shape[1]
                ref[index, end - (stop - start) : end] = result[
                    base + start : base + stop
                ].astype(jnp.bfloat16)


def backward_kernel(blocks, parts, held, *refs):
    grads = joined(refs[:blocks], refs[blocks : 2 * blocks])
    up_own, up_pair, down_own, down_pair, slope_ref = refs[2 * blocks : 2 * blocks + 5]
    held_refs = refs[2 * blocks + 5 : 2 * blocks + 5 + held]
    dpre_ref, *outs = refs[2 * blocks + 5 + held :]
    down = jnp.concatenate([down_own[0], down_pair[0]], 0)
    dpre = (dot(grads, down, 1, 1) * slope_ref[...].astype(jnp.float32)).astype(jnp.bfloat16)
    dpre_ref[...] = dpre
    up = jnp.concatenate([up_own[0], up_pair[0]], 0)
    spread(dot(dpre, up, 1, 0), blocks, parts, held_refs, outs)


def weight_kernel(blocks, *refs):
    rows = joined(refs[:blocks], refs[blocks : 2 * blocks])
    grads = joined(refs[2 * blocks : 3 * blocks], refs[3 * blocks : 4 * blocks])
    hidden_ref, dpre_ref, own_ref, pair_ref = refs[4 * blocks :]
    units = own_ref.shape[1]
    for index, (left_ref, right) in enumerate(((dpre_ref, rows), (hidden_ref, grads))):
        product = dot(left_ref[...], right, 0, 0)
        own_ref[index] = product[:units].astype(jnp.bfloat16)
        pair_ref[index] = product[units:].astype(jnp.bfloat16)


def total_kernel(local, *refs):
    own_refs = refs[:local]
    pair_refs = refs[local : 2 * local]
    out_refs = refs[2 * local :]
    for l in range(local):
        for index, ref in enumerate(out_refs):
            ref[l] = (
                own_refs[l][index].astype(jnp.float32) + pair_refs[l][index].astype(jnp.float32)
            ).astype(jnp.bfloat16)


def summed(refs):
    total = refs[0][0].astype(jnp.float32)
    for ref in refs[1:]:
        total = total + ref[0].astype(jnp.float32)
    return total.astype(jnp.bfloat16)


def finish_kernel(groups, *refs):
    outs = refs[sum(count for counts in groups for count in counts) :]
    cap = outs[0].shape[0] // len(groups)
    used = 0
    for l, counts in enumerate(groups):
        sums = []
        for count in counts:
            sums.append(summed(refs[used : used + count]))
            used += count
        low = jnp.concatenate(sums, 0)
        for index, out in enumerate(outs):
            out[l * cap : (l + 1) * cap] = low[index * cap : (index + 1) * cap]


def output_kernel(count, *refs):
    tok_ref, cot_ref, target_ref, weight_ref, alive_ref, out_ref, gating_ref = refs[-7:]
    results = jnp.concatenate(
        [summed(refs[:count])] + [ref[...] for ref in refs[count:-7]], 0
    )
    toks = tok_ref.shape[0]
    row = lax.broadcasted_iota(jnp.int32, (toks, toks), 0)
    same = row == lax.broadcasted_iota(jnp.int32, (toks, toks), 1)
    total = tok_ref[...].astype(jnp.float32)
    cot = cot_ref[...].astype(jnp.float32)
    for k in range(target_ref.shape[1]):
        picked = dot(one_hot(target_ref[:, k : k + 1], results.shape[0]), results, 1, 0)
        total = total + weight_ref[:, k : k + 1] * picked
        column = alive_ref[...] * jnp.sum(cot * picked, axis=1, keepdims=True)
        gating_ref[k : k + 1, :] = jnp.sum(jnp.where(same, column, 0.0), axis=0, keepdims=True)
    out_ref[...] = total.astype(jnp.bfloat16)


def input_kernel(count, *refs):
    tok_ref, cot_ref, target_ref, alive_ref, out_ref = refs[-5:]
    grads = jnp.concatenate([summed(refs[:count])] + [ref[...] for ref in refs[count:-5]], 0)
    hot = one_hot(target_ref[:, 0:1], grads.shape[0])
    for k in range(1, target_ref.shape[1]):
        hot = hot + one_hot(target_ref[:, k : k + 1], grads.shape[0])
    dnorm = alive_ref[...] * dot(hot, grads, 1, 0)
    normed, inv_scale = normalize(tok_ref[...])
    inner = jnp.mean(dnorm * normed, axis=1, keepdims=True)
    change = dnorm - jnp.mean(dnorm, axis=1, keepdims=True) - normed * inner
    out_ref[...] = (cot_ref[...].astype(jnp.float32) + inv_scale * change).astype(jnp.bfloat16)


def whole(array):
    rank = len(array.shape)
    return pl.BlockSpec(array.shape, lambda *_: (0,) * rank)


def part(array, index):
    rank = len(array.shape)
    return pl.BlockSpec((1,) + array.shape[1:], lambda *_: (index,) + (0,) * (rank - 1))


def slab(array, index, rows):
    return pl.BlockSpec((rows, array.shape[1]), lambda *_: (index, 0))


def spec_of(item):
    if not isinstance(item, tuple):
        return whole(item)
    return part(*item) if len(item) == 2 else slab(*item)


def run(kernel, inputs, outs):
    arrays = [item[0] if isinstance(item, tuple) else item for item in inputs]
    specs = [spec_of(item) for item in inputs]
    outs = [jax.ShapeDtypeStruct(shape, dtype) for shape, dtype in outs]
    return pl.pallas_call(
        kernel,
        out_shape=outs,
        grid=(1,),
        in_specs=specs,
        out_specs=[whole(out) for out in outs],
        compiler_params=pltpu.CompilerParams(vmem_limit_bytes=24 << 20),
    )(*arrays)


def body(
    tokens, cotangent, gate_weights, expert_ids, segments, keep_counts, expand_weight, reduce_weight
):
    toks, width = tokens.shape
    top = expert_ids.shape[1]
    groups = lax.axis_size("dp")
    planes = lax.axis_size("expert")
    local, units, _ = expand_weight.shape
    cap = top * toks // (planes * local)
    blocks = groups // 2
    bits = [1 << bit for bit in range(1, groups.bit_length() - 1)]
    block_rows = planes * cap
    low = jnp.bfloat16

    def swap(values, mask):
        return lax.ppermute(values, "dp", [(i, i ^ mask) for i in range(groups)])

    def cross(pieces):
        away = []
        for s, piece in enumerate(pieces, 1):
            away.append(lax.ppermute(piece, "expert", [(i, i ^ s) for i in range(planes)]))
        return away

    def order_of(name):
        shift = turns[name] % len(bits)
        return bits[shift:] + bits[:shift]

    def gather(name, own):
        held = {0: own}
        for bit in order_of(name):
            for block in sorted(held):
                held[block | bit] = swap(held[block], bit)
        return [held[2 * index] for index in range(blocks)]

    def part_of(name, start, stop):
        bit = order_of(name)[0] // 2
        slots = tuple((block | bit, block) for block in range(blocks) if not block & bit)
        return start, stop, slots

    def scatter(name, send, keep):
        order = order_of(name)
        bit = order[0]
        arrived = swap(send, bit)
        terms = {
            2 * slots[1]: [(keep, index), (arrived, index)]
            for index, slots in enumerate(part_of(name, 0, 0)[2])
        }
        for bit in order[1:]:
            leaving = [block for block in sorted(terms) if block & bit]
            sums = [
                run(add_kernel, terms[block], [((1,) + send.shape[1:], low)])[0]
                for block in leaving
            ]
            sums = sums[0] if len(sums) == 1 else jnp.concatenate(sums, 0)
            arrived = swap(sums, bit)
            for index, block in enumerate(leaving):
                terms[block ^ bit].append((arrived, index))
                del terms[block]
        return terms[0]

    me = lax.axis_index("expert").astype(jnp.int32).reshape(1)
    others = planes - 1
    near_parts = 1 if merge_near else 2
    feature_parts = 1 if merge_features else local
    grad_parts = local if split_grads else 1
    sources = [gate_weights.T, expert_ids.T, segments, keep_counts, tokens, cotangent]
    routed = pl.pallas_call(
        functools.partial(route_kernel, planes, local),
        out_shape=[jax.ShapeDtypeStruct((2 * local * cap // near_parts, width), low)] * near_parts
        + [jax.ShapeDtypeStruct((local * cap // feature_parts, width), low)]
        * (feature_parts * others)
        + [jax.ShapeDtypeStruct((local * cap // grad_parts, width), low)] * (grad_parts * others)
        + [
            jax.ShapeDtypeStruct((toks, top), jnp.int32),
            jax.ShapeDtypeStruct((toks, top), jnp.float32),
            jax.ShapeDtypeStruct((toks, 1), jnp.float32),
        ],
        in_specs=[pl.BlockSpec(memory_space=pltpu.SMEM)]
        + [pl.BlockSpec(memory_space=pltpu.HBM)] * len(sources),
        scratch_shapes=[pltpu.VMEM(source.shape, source.dtype) for source in sources]
        + [pltpu.SemaphoreType.DMA((len(sources),))],
        compiler_params=pltpu.CompilerParams(vmem_limit_bytes=24 << 20),
        name="route",
    )(me, *[pltpu.with_memory_space_constraint(source, pltpu.HBM) for source in sources])
    away = routed[near_parts:-3]
    target, weight, alive = routed[-3:]
    up_pair = swap(expand_weight, 1)
    down_pair = swap(reduce_weight, 1)

    far = others * cap
    if merge_near:
        near = gather("px", routed[0])
        near_features = [[(block, l, cap) for block in near] for l in range(local)]
        near_grads = [[(block, local + l, cap) for block in near] for l in range(local)]
    else:
        near_blocks = gather("px", routed[0]), gather("pg", routed[1])
        near_features, near_grads = [
            [[(block, l, cap) for block in held] for l in range(local)] for held in near_blocks
        ]

    def collect(name, pieces, split, merge):
        count = local if split else 1
        owns = []
        for index in range(count):
            arrived = cross(pieces[index * others : (index + 1) * others])
            owns += run(
                functools.partial(join_kernel, others, cap, merge),
                arrived,
                [((local * far if merge else far, width), low)]
                * (1 if merge else local // count),
            )
        if merge:
            held = gather(name, owns[0])
            return [[(block, l, far) for block in held] for l in range(local)]
        return [gather(f"{name}{l}", owns[l]) for l in range(local)]

    features = collect("x", away[: feature_parts * others], not merge_features, merge_features)
    features = [near_features[l] + features[l] for l in range(local)]
    grads = collect("g", away[feature_parts * others :], split_grads, merge_grads)
    grads = [near_grads[l] + grads[l] for l in range(local)]

    rows = blocks * block_rows
    flat = ((rows, 2 * units), low)

    def outs_of(l, parts):
        sizes = [(l + 1) * cap] + [stop - start for start, stop, _ in parts[1:]]
        return [((blocks // 2, size, width), low) for size in sizes for _ in range(2)]

    hiddens, slopes, result_terms, held = [], [], [], []
    for l in range(local):
        parts = [part_of("py", 0, cap), part_of(f"y{l}", cap, block_rows)]
        hidden, slope, *sends = run(
            functools.partial(forward_kernel, blocks, parts, len(held)),
            features[l]
            + [(expand_weight, l), (up_pair, l), (reduce_weight, l), (down_pair, l)]
            + held,
            [flat, flat] + outs_of(l, parts),
        )
        hiddens.append(hidden)
        slopes.append(slope)
        held = sends[:2]
        result_terms.append([scatter(f"y{l}", sends[2], sends[3])])
    near_results = scatter("py", *held)
    dpres, input_terms, held = [], [], []
    for l in range(local):
        parts = [part_of("pd", 0, cap)]
        if split_inputs:
            half = cap + others * cap // 32 * 16
            named = [(f"d{l}0", cap, half), (f"d{l}1", half, block_rows)]
        else:
            named = [(f"d{l}", cap, block_rows)]
        parts += [part_of(*item) for item in named]
        dpre, *sends = run(
            functools.partial(backward_kernel, blocks, parts, len(held)),
            grads[l]
            + [(expand_weight, l), (up_pair, l), (reduce_weight, l), (down_pair, l), slopes[l]]
            + held,
            [flat] + outs_of(l, parts),
        )
        dpres.append(dpre)
        held = sends[:2]
        input_terms.append(
            [
                scatter(item[0], *sends[2 * index + 2 : 2 * index + 4])
                for index, item in enumerate(named)
            ]
        )
    near_inputs = scatter("pd", *held)
    owns, pairs = [], []
    for l in range(local):
        own, pair = run(
            functools.partial(weight_kernel, blocks),
            features[l] + grads[l] + [hiddens[l], dpres[l]],
            [((2, units, width), low)] * 2,
        )
        owns.append(own)
        pairs.append(swap(pair, 1))
    expand_grad, reduce_grad = run(
        functools.partial(total_kernel, local), owns + pairs, [(expand_weight.shape, low)] * 2
    )

    def finish(terms_list):
        groups = [[len(terms) for terms in parts] for parts in terms_list]
        outs = run(
            functools.partial(finish_kernel, groups),
            [item for parts in terms_list for terms in parts for item in terms],
            [((len(terms_list) * cap, width), low)] * others,
        )
        return cross(outs)

    if split_results:
        returned = [finish([result_terms[l]]) for l in range(local)]
        returned = [returned[l][s] for s in range(others) for l in range(local)]
    else:
        returned = finish(result_terms)
    output, gating_grad = run(
        functools.partial(output_kernel, len(near_results)),
        near_results + returned + [tokens, cotangent, target, weight, alive],
        [(tokens.shape, low), ((top, toks), jnp.float32)],
    )
    back = [finish([input_terms[l]]) for l in range(local)]
    (tokens_grad,) = run(
        functools.partial(input_kernel, len(near_inputs)),
        near_inputs
        + [back[l][s] for s in range(others) for l in range(local)]
        + [tokens, cotangent, target, alive],
        [(tokens.shape, low)],
    )
    return (output, tokens_grad, gating_grad.T, expand_grad, reduce_grad)


def solution(mesh):
    rows = P(("dp", "expert"), None)
    weights = P("expert", "dp", None)

    return jax.shard_map(
        body,
        mesh=mesh,
        in_specs=(rows,) * 6 + (weights,) * 2,
        out_specs=(rows,) * 3 + (weights,) * 2,
        check_vma=False,
    )
```
